32 devices in a mesh: chan: 2 (over y), seq: 8 (over z, core), dp: 2 (over x).
Axes of the slice: x: 2, y: 2, z: 4, core: 2. Of those that a mesh axis runs over, the one named last changes fastest.
Arguments:
- queries: bfloat16 [2, 2, 1024, 2048], P('dp', 'chan', 'seq'), may hold values from -8 to 8
- keys: bfloat16 [2, 2, 1024, 2048], P('dp', 'chan', 'seq'), may hold values from -8 to 8
- values: bfloat16 [2, 2, 1024, 2048], P('dp', 'chan', 'seq'), may hold values from -6 to 6
- out_grad: bfloat16 [2, 2, 1024, 2048], P('dp', 'chan', 'seq'), may hold values from -6 to 6
- cross_bias: float32 [16], replicated, may hold values from -2 to 2
- lengths: int32 [2], P('dp'), may hold values from 256 to 1024
Outputs:
- query_grad: bfloat16 [2, 2, 1024, 2048], P('dp', 'chan', 'seq')
- key_grad: bfloat16 [2, 2, 1024, 2048], P('dp', 'chan', 'seq')
- value_grad: bfloat16 [2, 2, 1024, 2048], P('dp', 'chan', 'seq')
- bias_grad: float32 [16], replicated
The draws below stay inside these ranges and needn't reach their ends.
Inputs may be any that keep to these rules, and one draw needn't show every extreme that they name: Frames of conversation b from lengths[b] on are padding in both channels.
All inputs are finite; a program needn't handle non-finite values.
Results may differ from the reference program's by a relative error of at most 0.011.
Values may be sent and summed in bfloat16 or wider, within the bound.
No kernel may reach another device: no remote copies, remote signals or barrier semaphores. Data moves between devices by JAX's collectives and lax.ppermute only.
A program may use at most 128 MiB of HBM per device.

```python
import math
import jax
import jax.numpy as jnp
from jax import lax

TOK_DEV = 128
HEADS = 16
HEAD_DIM = 128
LOOKBACK = 6
FRAMES = 1024
CONVS = 2
N_SEQ = 8


def aligned_pattern(key):
    array_shape = (CONVS, 2, FRAMES, HEADS * HEAD_DIM)
    sign_table = jnp.where(jax.random.bernoulli(jax.random.fold_in(key, 11), 0.5, array_shape), 1.0, -1.0)
    position = jnp.arange(FRAMES, dtype=jnp.int32)
    marked = position % (2 * TOK_DEV) == TOK_DEV // 2
    level = (position // (2 * TOK_DEV) % 3).astype(jnp.float32)
    strength = 5.0 + 1.5 * level
    return (sign_table, marked, strength)


def background_draw(key, salt):
    array_shape = (CONVS, 2, FRAMES, HEADS * HEAD_DIM)
    return jnp.clip(jax.random.normal(jax.random.fold_in(key, salt), array_shape, jnp.float32), -5.0, 5.0)


def draw_queries(key, part):
    background = background_draw(key, 21)
    sign_table, marked, strength = aligned_pattern(key)
    planted = sign_table * strength[None, None, :, None]
    return jnp.where(marked[None, None, :, None], planted, background).astype(jnp.bfloat16)


def draw_keys(key, part):
    background = background_draw(key, 31)
    sign_table, marked, strength = aligned_pattern(key)
    planted = sign_table * strength[None, None, :, None]
    next_marked = jnp.roll(marked, -1)
    next_strength = jnp.roll(strength, -1)
    shrink = 1.0 - 2.0 / (next_strength * next_strength * HEAD_DIM ** 0.5)
    neighbour = jnp.roll(sign_table, -1, axis=2) * (next_strength * shrink)[None, None, :, None]
    result = jnp.where(next_marked[None, None, :, None], neighbour, background)
    result = jnp.where(marked[None, None, :, None], planted, result)
    return result.astype(jnp.bfloat16)


def shard_levels(rng, extent, pieces, low, high):
    def one(dim, blocks):
        heights = jax.random.uniform(jax.random.fold_in(jax.random.fold_in(rng, 6), dim), (blocks,), jnp.float32, low / len(pieces), high / len(pieces))
        return jnp.repeat(jnp.exp(heights), extent[dim] // blocks).reshape((-1,) + (1,) * (len(extent) - dim - 1))

    gain = one(*pieces[0])
    for cut in pieces[1:]:
        gain = gain * one(*cut)
    return gain


def noise(rng, extent, width, most, shards=(), kind=jnp.bfloat16):
    loudness = shard_levels(rng, extent, shards, -0.22, 0.18) if shards else 1.0
    entries = jax.random.normal(rng, extent, jnp.float32) * width * loudness
    return jnp.minimum(jnp.maximum(entries, -most), most).astype(kind)


def setup_inputs(seed: int = 0) -> dict:
    streams_of = jax.random.split(jax.random.key(seed), 7)
    return {
        "queries": draw_queries(jax.random.fold_in(streams_of[6], 71), 0),
        "keys": draw_keys(jax.random.fold_in(streams_of[6], 71), 0),
        "values": noise(streams_of[2], (CONVS, 2, FRAMES, HEADS * HEAD_DIM), 1.0, 6.0, ((0, 2), (1, 2), (2, 8))),
        "out_grad": noise(streams_of[3], (CONVS, 2, FRAMES, HEADS * HEAD_DIM), 1.0, 6.0, ((0, 2), (1, 2), (2, 8))),
        "cross_bias": jnp.clip(jax.random.uniform(streams_of[4], (HEADS,), jnp.float32, -2.0, 2.0), -2.0, 2.0),
        "lengths": jax.random.randint(streams_of[5], (CONVS,), FRAMES // 4, FRAMES + 1).astype(jnp.int32),
    }


NEG_FILL = -1e+30

def reference(queries, keys, values, out_grad, cross_bias, lengths):
    feature_width = HEADS * HEAD_DIM
    front_rows = LOOKBACK * TOK_DEV
    window_rows = (LOOKBACK + 1) * TOK_DEV
    root_scale = 1.0 / math.sqrt(HEAD_DIM)
    highest = lax.Precision.HIGHEST

    def conversation(packed):
        query_all, key_all, value_all, grad_all, dialog_length = packed
        key_pad = jnp.pad(key_all, ((0, 0), (front_rows, 0), (0, 0)))
        value_pad = jnp.pad(value_all, ((0, 0), (front_rows, 0), (0, 0)))

        def block_step(carried, block_index):
            key_sum, value_sum, bias_sum = carried
            first_frame = (block_index * TOK_DEV).astype(jnp.int32)
            query_block = lax.dynamic_slice_in_dim(query_all, first_frame, TOK_DEV, 1)
            grad_block = lax.dynamic_slice_in_dim(grad_all, first_frame, TOK_DEV, 1)
            key_block = lax.dynamic_slice_in_dim(key_pad, first_frame, window_rows, 1)
            value_block = lax.dynamic_slice_in_dim(value_pad, first_frame, window_rows, 1)
            query_heads = query_block.reshape(2 * TOK_DEV, HEADS, HEAD_DIM).astype(jnp.float32)
            grad_heads = grad_block.reshape(2 * TOK_DEV, HEADS, HEAD_DIM).astype(jnp.float32)
            key_heads = key_block.reshape(2 * window_rows, HEADS, HEAD_DIM).astype(jnp.float32)
            value_heads = value_block.reshape(2 * window_rows, HEADS, HEAD_DIM).astype(jnp.float32)
            query_frame = jnp.tile(first_frame + jnp.arange(TOK_DEV, dtype=jnp.int32), 2)
            key_frame = jnp.tile(first_frame - front_rows + jnp.arange(window_rows, dtype=jnp.int32), 2)
            tower_index = jnp.arange(2 * TOK_DEV, dtype=jnp.int32) // TOK_DEV
            key_channel = jnp.arange(2 * window_rows, dtype=jnp.int32) // window_rows
            partner = (tower_index[:, None] != key_channel[None, :]).astype(jnp.float32)
            allowed = (key_frame[None, :] > query_frame[:, None] - front_rows) & (key_frame[None, :] <= query_frame[:, None])
            allowed = allowed & (key_frame[None, :] >= 0) & (key_frame[None, :] < dialog_length)
            allowed = allowed & (query_frame[:, None] < dialog_length)
            scores = jnp.einsum('phd,shd->hps', query_heads, key_heads, precision=highest) * root_scale
            scores = scores + cross_bias[:, None, None] * partner[None]
            scores = jnp.where(allowed[None], scores, NEG_FILL)
            row_max = lax.optimization_barrier(jnp.max(scores, axis=2))
            row_total = lax.optimization_barrier(jnp.sum(jnp.where(allowed[None], jnp.exp(scores - row_max[:, :, None]), 0.0), axis=2))
            log_norm = row_max + jnp.log(jnp.where(row_total > 0.0, row_total, 1.0))
            weights = jnp.where(allowed[None], jnp.exp(scores - log_norm[:, :, None]), 0.0)
            weight_grad = jnp.einsum('phd,shd->hps', grad_heads, value_heads, precision=highest)
            row_delta = lax.optimization_barrier(jnp.sum(weights * weight_grad, axis=2))
            score_grad = weights * (weight_grad - row_delta[:, :, None])
            weight_low = lax.optimization_barrier(weights.astype(jnp.bfloat16)).astype(jnp.float32)
            score_low = lax.optimization_barrier(score_grad.astype(jnp.bfloat16)).astype(jnp.float32)
            query_term = jnp.einsum('hps,shd->phd', score_low, key_heads, precision=highest) * root_scale
            key_term = jnp.einsum('hps,phd->shd', score_low, query_heads, precision=highest) * root_scale
            value_term = jnp.einsum('hps,phd->shd', weight_low, grad_heads, precision=highest)
            bias_term = lax.optimization_barrier(jnp.sum(score_grad * partner[None], axis=(1, 2)))
            key_old = lax.dynamic_slice_in_dim(key_sum, first_frame, window_rows, 1)
            value_old = lax.dynamic_slice_in_dim(value_sum, first_frame, window_rows, 1)
            key_sum = lax.dynamic_update_slice_in_dim(key_sum, key_old + key_term.reshape(2, window_rows, feature_width), first_frame, 1)
            value_sum = lax.dynamic_update_slice_in_dim(value_sum, value_old + value_term.reshape(2, window_rows, feature_width), first_frame, 1)
            query_out = query_term.reshape(2, TOK_DEV, feature_width).astype(jnp.bfloat16)
            return ((key_sum, value_sum, bias_sum + bias_term), query_out)
        initial = (jnp.zeros((2, front_rows + FRAMES, feature_width), jnp.float32), jnp.zeros((2, front_rows + FRAMES, feature_width), jnp.float32), jnp.zeros((HEADS,), jnp.float32))
        finals, query_blocks = lax.scan(block_step, initial, jnp.arange(N_SEQ, dtype=jnp.int32))
        key_sum, value_sum, bias_sum = finals
        query_whole = jnp.transpose(query_blocks, (1, 0, 2, 3)).reshape(2, FRAMES, feature_width)
        return (query_whole, key_sum[:, front_rows:].astype(jnp.bfloat16), value_sum[:, front_rows:].astype(jnp.bfloat16), bias_sum)
    results = lax.map(conversation, (queries, keys, values, out_grad, lengths))
    return (results[0], results[1], results[2], lax.optimization_barrier(jnp.sum(results[3], axis=0)))
```

```python
import functools
import math

import jax
import jax.numpy as jnp
from jax import lax
from jax.experimental import pallas as pl
from jax.experimental.pallas import tpu as pltpu
from jax.sharding import PartitionSpec as P

LOOKBACK = 6
NEG_FILL = -1e30
EXTRA = 8


def pack_kernel(copies, q_ref, k_ref, v_ref, g_ref, send_ref, sems):
    width = send_ref.shape[3]
    sources = (q_ref, k_ref, v_ref, g_ref)
    started = []
    for dest in range(send_ref.shape[0]):
        head = dest // copies
        for kind, source in enumerate(sources):
            copy = pltpu.make_async_copy(
                source.at[:, pl.ds(head * width, width)], send_ref.at[dest, kind], sems.at[dest, kind]
            )
            copy.start()
            started.append(copy)
    for copy in started:
        copy.wait()


def unpack_kernel(home_ref, q_ref, k_ref, v_ref, sems):
    heads = home_ref.shape[0]
    rows, width = q_ref.shape[0], home_ref.shape[2]
    started = []
    for head in range(heads):
        for kind, target in enumerate((q_ref, k_ref, v_ref)):
            copy = pltpu.make_async_copy(
                home_ref.at[head, pl.ds(kind * rows, rows)],
                target.at[:, pl.ds(head * width, width)],
                sems.at[head, kind],
            )
            copy.start()
            started.append(copy)
    for copy in started:
        copy.wait()


def head_kernel(copies, length_ref, place_ref, bias_ref, got_ref, out_ref, kt_ref, s_ref, d_ref, dk_ref, dv_ref, bias_acc):
    devices, _, rows, width = got_ref.shape
    blocks = devices // 2
    both = 2 * rows
    root_scale = 1.0 / math.sqrt(width)
    log2_scale = root_scale * math.log2(math.e)
    length = length_ref[0]
    bias = bias_ref[place_ref[0]] * math.log2(math.e)
    part = place_ref[1]

    def pair(kind, block):
        return jnp.concatenate([got_ref[block, kind], got_ref[blocks + block, kind]], axis=0)

    def dot(left, right, contract):
        return lax.dot_general(left, right, (contract, ((), ())), preferred_element_type=jnp.float32)

    column = lax.broadcasted_iota(jnp.int32, (1, both), 1)
    own = [jnp.where((column // rows) == c, 0.0, bias) for c in range(2)]
    key_row = lax.broadcasted_iota(jnp.int32, (rows, both), 0)
    query_column = lax.broadcasted_iota(jnp.int32, (rows, both), 1) % rows
    causal = key_row <= query_column
    in_reach = key_row > query_column

    out_ref[...] = jnp.zeros_like(out_ref)
    dk_ref[...] = jnp.zeros_like(dk_ref)
    dv_ref[...] = jnp.zeros_like(dv_ref)
    bias_acc[...] = jnp.zeros_like(bias_acc)

    def fold(tile, op):
        return op(tile.reshape(tile.shape[0] // 8, 8, tile.shape[1]), axis=0)

    def row_block(block, tiles):
        queries = pair(0, block)
        grads = pair(3, block)
        first = block - (tiles - 1)
        peak = jnp.full((8, both), NEG_FILL, jnp.float32)
        for t in range(tiles):
            raw = dot(pair(1, first + t), queries, ((1,), (1,)))
            for c in range(2):
                tile = raw[c * rows : (c + 1) * rows] * log2_scale + own[c]
                if t == tiles - 1:
                    tile = jnp.where(causal, tile, NEG_FILL)
                if tiles == LOOKBACK + 1 and t == 0:
                    tile = jnp.where(in_reach, tile, NEG_FILL)
                s_ref[t, c * rows : (c + 1) * rows] = tile
                peak = jnp.maximum(peak, fold(tile, jnp.max))
        peak = jnp.max(peak, axis=0, keepdims=True)
        total = jnp.zeros((8, both), jnp.float32)
        moment = jnp.zeros((8, both), jnp.float32)
        for t in range(tiles):
            weight_grad = dot(pair(2, first + t), grads, ((1,), (1,)))
            d_ref[t] = weight_grad
            power = jnp.exp2(s_ref[t] - peak)
            s_ref[t] = power
            total = total + fold(power, jnp.sum)
            moment = moment + fold(power * weight_grad, jnp.sum)
        total = jnp.sum(total, axis=0, keepdims=True)
        moment = jnp.sum(moment, axis=0, keepdims=True)
        frame = block * rows + column % rows
        live = frame < length
        if copies > 1:
            live = live & ((column * copies) // both == part)
        inverse = jnp.where(live, 1.0 / total, 0.0)
        delta = moment * inverse
        query_sum = jnp.zeros((width, both), jnp.float32)
        cross = jnp.zeros((8, rows), jnp.float32)
        for t in range(tiles):
            weights = s_ref[t] * inverse
            score_grad = weights * (d_ref[t] - delta)
            cross = cross + fold(score_grad[:rows, rows:], jnp.sum) + fold(score_grad[rows:, :rows], jnp.sum)
            weight_low = weights.astype(jnp.bfloat16)
            score_low = score_grad.astype(jnp.bfloat16)
            dv_ref[first + t] += dot(weight_low, grads, ((1,), (0,)))
            dk_ref[first + t] += dot(score_low, queries, ((1,), (0,)))
            query_sum = query_sum + dot(kt_ref[first + t], score_low, ((1,), (0,)))
        bias_acc[...] += cross
        query_grad = (query_sum.T * root_scale).astype(jnp.bfloat16)
        out_ref[block, 0:rows] = query_grad[:rows]
        out_ref[blocks + block, 0:rows] = query_grad[rows:]

    for block in range(blocks):
        kt_ref[block] = pair(1, block).T

    live_blocks = jnp.minimum((length + rows - 1) // rows, blocks)
    for block in range(min(LOOKBACK, blocks)):
        @pl.when(block < live_blocks)
        def _():
            row_block(block, block + 1)

    if blocks > LOOKBACK:
        def step(block, carried):
            row_block(block, LOOKBACK + 1)
            return carried

        lax.fori_loop(LOOKBACK, live_blocks, step, 0)

    for block in range(blocks):
        key_grad = (dk_ref[block] * root_scale).astype(jnp.bfloat16)
        value_grad = dv_ref[block].astype(jnp.bfloat16)
        for c in range(2):
            out_ref[c * blocks + block, rows : 2 * rows] = key_grad[c * rows : (c + 1) * rows]
            out_ref[c * blocks + block, 2 * rows : 3 * rows] = value_grad[c * rows : (c + 1) * rows]

    whole = jnp.sum(jnp.sum(bias_acc[...], axis=0, keepdims=True), axis=1, keepdims=True)
    whole = jnp.broadcast_to(whole, (1, width))
    high = whole.astype(jnp.bfloat16)
    rest = whole - high.astype(jnp.float32)
    middle = rest.astype(jnp.bfloat16)
    low = (rest - middle.astype(jnp.float32)).astype(jnp.bfloat16)
    lane = lax.broadcasted_iota(jnp.int32, (1, width), 1)
    pieces = jnp.where(
        lane == 0,
        high.astype(jnp.float32),
        jnp.where(lane == 1, middle.astype(jnp.float32), jnp.where(lane == 2, low.astype(jnp.float32), 0.0)),
    ).astype(jnp.bfloat16)
    pieces = jnp.broadcast_to(pieces, (EXTRA, width))
    for dest in range(devices):
        out_ref[dest, 3 * rows : 3 * rows + EXTRA] = pieces


def summed_over(value, axis):
    count = lax.axis_size(axis)
    if count & (count - 1):
        return lax.psum(value, axis)
    step = 1
    while step < count:
        pairs = [(source, source ^ step) for source in range(count)]
        value = value + lax.ppermute(value, axis, pairs)
        step *= 2
    return value


def shards(queries, keys, values, out_grad, cross_bias, lengths):
    rows, features = queries.shape[2:]
    heads = cross_bias.shape[0]
    width = features // heads
    blocks = lax.axis_size("seq")
    devices = lax.axis_size("chan") * blocks
    copies = devices // heads
    place = lax.axis_index("chan") * blocks + lax.axis_index("seq")
    vmem = pl.BlockSpec(memory_space=pltpu.VMEM)
    smem = pl.BlockSpec(memory_space=pltpu.SMEM)
    anywhere = pl.BlockSpec(memory_space=pl.ANY)

    send = pl.pallas_call(
        functools.partial(pack_kernel, copies),
        out_shape=jax.ShapeDtypeStruct((devices, 4, rows, width), queries.dtype),
        in_specs=[anywhere] * 4,
        out_specs=vmem,
        scratch_shapes=[pltpu.SemaphoreType.DMA((devices, 4))],
        name="pack",
    )(queries[0, 0], keys[0, 0], values[0, 0], out_grad[0, 0])
    got = lax.all_to_all(send, ("chan", "seq"), 0, 0, tiled=True)

    payload = 3 * rows + EXTRA
    both = 2 * rows
    tiles = min(LOOKBACK + 1, blocks)
    back = pl.pallas_call(
        functools.partial(head_kernel, copies),
        out_shape=jax.ShapeDtypeStruct((devices, payload, width), queries.dtype),
        in_specs=[smem, smem, smem, vmem],
        out_specs=vmem,
        scratch_shapes=[
            pltpu.VMEM((blocks, width, both), jnp.bfloat16),
            pltpu.VMEM((tiles, both, both), jnp.float32),
            pltpu.VMEM((tiles, both, both), jnp.float32),
            pltpu.VMEM((blocks, both, width), jnp.float32),
            pltpu.VMEM((blocks, both, width), jnp.float32),
            pltpu.VMEM((8, rows), jnp.float32),
        ],
        name="head",
    )(lengths, jnp.stack([place // copies, place % copies]).astype(jnp.int32), cross_bias, got)
    home = lax.all_to_all(back, ("chan", "seq"), 0, 0, tiled=True)

    pieces = home[:, 3 * rows, :3].astype(jnp.float32)
    if copies > 1:
        pieces = jnp.sum(pieces.reshape(heads, copies, 3), axis=1)
        home = jnp.sum(home.reshape(heads, copies, payload, width).astype(jnp.float32), axis=1).astype(queries.dtype)
    bias_out = summed_over(pieces[:, 0] + pieces[:, 1] + pieces[:, 2], "dp")
    flat = jax.ShapeDtypeStruct((rows, features), queries.dtype)
    grads = pl.pallas_call(
        unpack_kernel,
        out_shape=(flat, flat, flat),
        in_specs=[vmem],
        out_specs=(anywhere, anywhere, anywhere),
        scratch_shapes=[pltpu.SemaphoreType.DMA((heads, 3))],
        name="unpack",
    )(home)
    return tuple(grad[None, None] for grad in grads) + (bias_out,)


def solution(mesh):
    placed = P("dp", "chan", "seq", None)
    return jax.shard_map(
        shards,
        mesh=mesh,
        in_specs=(placed, placed, placed, placed, P(), P("dp")),
        out_specs=(placed, placed, placed, P()),
        check_vma=False,
    )
```

```python
import functools
import math

import jax
import jax.numpy as jnp
from jax import lax
from jax.experimental import pallas as pl
from jax.experimental.pallas import tpu as pltpu
from jax.sharding import PartitionSpec as P

LOOKBACK = 6
NEG_FILL = -1e30
EXTRA = 8
PACK_BYTES = 12 << 20
HEAD_BYTES = 24 << 20


def stages(devices):
    seats = [0, 1, devices // 2, devices // 2 + 1]
    lanes = [2 * step for step in range(devices // 4)]
    return seats, lanes


def run_all(copies):
    for copy in copies:
        copy.start()
    for copy in copies:
        copy.wait()


def pack_kernel(copies, place_ref, q_ref, k_ref, v_ref, g_ref, *refs):
    sems = refs[-1]
    seats, lanes = stages(sems.shape[0])
    by_lane, by_seat = refs[: len(lanes)], refs[len(lanes) : -1]
    width = by_lane[0].shape[-1]
    started = []
    for i, lane in enumerate(lanes):
        for j, seat in enumerate(seats):
            head = (place_ref[0] ^ (lane + seat)) // copies
            columns = pl.ds(pl.multiple_of(head * width, width), width)
            for kind, source in enumerate((q_ref, k_ref, v_ref, g_ref)):
                target = by_lane[i].at[j, kind] if kind < 2 else by_seat[j].at[i, kind - 2]
                started.append(pltpu.make_async_copy(source.at[:, columns], target, sems.at[len(seats) * i + j, kind]))
    run_all(started)


def unpack_kernel(copies, place_ref, *refs):
    sems, home_a, home_b = refs[-1], refs[-3], refs[-2]
    outs = refs[-6:-3]
    devices = sems.shape[0]
    seats, lanes = stages(devices)
    arrived = gathered(place_ref[0], refs[:-6], (home_a, home_b), sems, seats, lanes)
    run_all(arrived)
    half = home_b.shape[1] // 3
    width = home_b.shape[2]
    for head in range(devices // copies):
        for kind, out in enumerate(outs):
            for part, home in enumerate((home_a, home_b)):
                rows = pl.ds(kind * half, half)
                value = home[head * copies, rows]
                if copies > 1:
                    value = value.astype(jnp.float32)
                    for other in range(1, copies):
                        value = value + home[head * copies + other, rows].astype(jnp.float32)
                out[part * half : (part + 1) * half, head * width : (head + 1) * width] = value.astype(out.dtype)


def gathered(place, refs, targets, sems, seats, lanes):
    first_a, last_a, first_b, last_b = split_refs(refs, seats, lanes)
    started = []
    for i, lane in enumerate(lanes):
        for j, seat in enumerate(seats):
            other = place ^ (lane + seat)
            source_a = first_a[i].at[0] if j == 0 else last_a[j - 1].at[i]
            source_b = first_b[j].at[0] if i == 0 else last_b[i - 1].at[j]
            started.append(pltpu.make_async_copy(source_a, targets[0].at[other], sems.at[len(seats) * i + j, 0]))
            started.append(pltpu.make_async_copy(source_b, targets[1].at[other], sems.at[len(seats) * i + j, 1]))
    return started


def split_refs(refs, seats, lanes):
    cuts = [len(lanes), len(seats) - 1, len(seats), len(lanes) - 1]
    pieces, start = [], 0
    for cut in cuts:
        pieces.append(refs[start : start + cut])
        start += cut
    return pieces


def head_kernel(copies, length_ref, place_ref, bias_ref, *refs):
    got_sems, send_sems = refs[-2], refs[-1]
    qk_ref, vg_ref, out_a, out_b, kt_ref, s_ref, d_ref, dk_ref, dv_ref, bias_acc = refs[-12:-2]
    devices, _, rows, width = qk_ref.shape
    seats, lanes = stages(devices)
    arrays = refs[:-12]
    inputs = arrays[: 2 * (len(seats) + len(lanes)) - 2]
    outputs = arrays[len(inputs) :]
    place = place_ref[0]
    arriving = gathered(place, inputs, (qk_ref, vg_ref), got_sems, seats, lanes)
    blocks = devices // 2
    half = rows // 2
    both = 2 * rows
    root_scale = 1.0 / math.sqrt(width)
    log2_scale = root_scale * math.log2(math.e)
    length = length_ref[0]
    bias = bias_ref[place // copies] * math.log2(math.e)
    part = place % copies

    def pair(kind, block):
        source, kind = (qk_ref, kind) if kind < 2 else (vg_ref, kind - 2)
        return jnp.concatenate([source[block, kind], source[blocks + block, kind]], axis=0)

    def put(kind, c, block, tile):
        out_a[c * blocks + block, kind * half : (kind + 1) * half] = tile[:half]
        out_b[c * blocks + block, kind * half : (kind + 1) * half] = tile[half:]

    def dot(left, right, contract):
        return lax.dot_general(left, right, (contract, ((), ())), preferred_element_type=jnp.float32)

    column = lax.broadcasted_iota(jnp.int32, (1, both), 1)
    own = [jnp.where((column // rows) == c, 0.0, bias) for c in range(2)]
    key_row = lax.broadcasted_iota(jnp.int32, (rows, both), 0)
    query_column = lax.broadcasted_iota(jnp.int32, (rows, both), 1) % rows
    causal = key_row <= query_column
    in_reach = key_row > query_column

    for copy in arriving:
        copy.start()
    out_a[...] = jnp.zeros_like(out_a)
    out_b[...] = jnp.zeros_like(out_b)
    dk_ref[...] = jnp.zeros_like(dk_ref)
    dv_ref[...] = jnp.zeros_like(dv_ref)
    bias_acc[...] = jnp.zeros_like(bias_acc)

    def fold(tile, op):
        return op(tile.reshape(tile.shape[0] // 8, 8, tile.shape[1]), axis=0)

    def row_block(block, tiles):
        queries = pair(0, block)
        grads = pair(3, block)
        first = block - (tiles - 1)
        peak = jnp.full((8, both), NEG_FILL, jnp.float32)
        for t in range(tiles):
            raw = dot(pair(1, first + t), queries, ((1,), (1,)))
            for c in range(2):
                tile = raw[c * rows : (c + 1) * rows] * log2_scale + own[c]
                if t == tiles - 1:
                    tile = jnp.where(causal, tile, NEG_FILL)
                if tiles == LOOKBACK + 1 and t == 0:
                    tile = jnp.where(in_reach, tile, NEG_FILL)
                s_ref[t, c * rows : (c + 1) * rows] = tile
                peak = jnp.maximum(peak, fold(tile, jnp.max))
        peak = jnp.max(peak, axis=0, keepdims=True)
        total = jnp.zeros((8, both), jnp.float32)
        moment = jnp.zeros((8, both), jnp.float32)
        for t in range(tiles):
            weight_grad = dot(pair(2, first + t), grads, ((1,), (1,)))
            d_ref[t] = weight_grad
            power = jnp.exp2(s_ref[t] - peak)
            s_ref[t] = power
            total = total + fold(power, jnp.sum)
            moment = moment + fold(power * weight_grad, jnp.sum)
        total = jnp.sum(total, axis=0, keepdims=True)
        moment = jnp.sum(moment, axis=0, keepdims=True)
        frame = block * rows + column % rows
        live = frame < length
        if copies > 1:
            live = live & ((column * copies) // both == part)
        inverse = jnp.where(live, 1.0 / total, 0.0)
        delta = moment * inverse
        query_sum = jnp.zeros((width, both), jnp.float32)
        cross = jnp.zeros((8, rows), jnp.float32)
        for t in range(tiles):
            weights = s_ref[t] * inverse
            score_grad = weights * (d_ref[t] - delta)
            cross = cross + fold(score_grad[:rows, rows:], jnp.sum) + fold(score_grad[rows:, :rows], jnp.sum)
            weight_low = weights.astype(jnp.bfloat16)
            score_low = score_grad.astype(jnp.bfloat16)
            dv_ref[first + t] += dot(weight_low, grads, ((1,), (0,)))
            dk_ref[first + t] += dot(score_low, queries, ((1,), (0,)))
            query_sum = query_sum + dot(kt_ref[first + t], score_low, ((1,), (0,)))
        bias_acc[...] += cross
        query_grad = (query_sum.T * root_scale).astype(jnp.bfloat16)
        put(0, 0, block, query_grad[:rows])
        put(0, 1, block, query_grad[rows:])

    for copy in arriving:
        copy.wait()
    for block in range(blocks):
        kt_ref[block] = pair(1, block).T

    live_blocks = jnp.minimum((length + rows - 1) // rows, blocks)
    for block in range(min(LOOKBACK, blocks)):
        @pl.when(block < live_blocks)
        def _():
            row_block(block, block + 1)

    if blocks > LOOKBACK:
        def step(block, carried):
            row_block(block, LOOKBACK + 1)
            return carried

        lax.fori_loop(LOOKBACK, live_blocks, step, 0)

    for block in range(blocks):
        key_grad = (dk_ref[block] * root_scale).astype(jnp.bfloat16)
        value_grad = dv_ref[block].astype(jnp.bfloat16)
        for c in range(2):
            put(1, c, block, key_grad[c * rows : (c + 1) * rows])
            put(2, c, block, value_grad[c * rows : (c + 1) * rows])

    whole = jnp.sum(jnp.sum(bias_acc[...], axis=0, keepdims=True), axis=1, keepdims=True)
    whole = jnp.broadcast_to(whole, (1, width))
    high = whole.astype(jnp.bfloat16)
    rest = whole - high.astype(jnp.float32)
    middle = rest.astype(jnp.bfloat16)
    low = (rest - middle.astype(jnp.float32)).astype(jnp.bfloat16)
    lane = lax.broadcasted_iota(jnp.int32, (1, width), 1)
    pieces = jnp.where(
        lane == 0,
        high.astype(jnp.float32),
        jnp.where(lane == 1, middle.astype(jnp.float32), jnp.where(lane == 2, low.astype(jnp.float32), 0.0)),
    ).astype(jnp.bfloat16)
    pieces = jnp.broadcast_to(pieces, (EXTRA, width))
    for dest in range(devices):
        out_a[dest, 3 * half : 3 * half + EXTRA] = pieces
    leaving = []
    for i, lane in enumerate(lanes):
        for j, seat in enumerate(seats):
            other = place ^ (lane + seat)
            index = len(seats) * i + j
            leaving.append(pltpu.make_async_copy(out_a.at[other], outputs[i].at[j], send_sems.at[index, 0]))
            leaving.append(pltpu.make_async_copy(out_b.at[other], outputs[len(lanes) + j].at[i], send_sems.at[index, 1]))
    run_all(leaving)


def summed_over(value, axis):
    count = lax.axis_size(axis)
    if count & (count - 1):
        return lax.psum(value, axis)
    step = 1
    while step < count:
        pairs = [(source, source ^ step) for source in range(count)]
        value = value + lax.ppermute(value, axis, pairs)
        step *= 2
    return value


def moved(value, mask):
    devices = lax.axis_size("chan") * lax.axis_size("seq")
    if mask == 0:
        return value
    return lax.ppermute(value, ("chan", "seq"), [(source, source ^ mask) for source in range(devices)])


def exchanged(by_lane, by_seat, seats, lanes):
    first_a = [moved(value, lane) for value, lane in zip(by_lane, lanes)]
    first_b = [moved(value, seat) for value, seat in zip(by_seat, seats)]
    last_b = [moved(jnp.stack([value[i] for value in first_b]), lanes[i]) for i in range(1, len(lanes))]
    last_a = [moved(jnp.stack([value[j] for value in first_a]), seats[j]) for j in range(1, len(seats))]
    return first_a, last_a, first_b, last_b


def shards(queries, keys, values, out_grad, cross_bias, lengths):
    rows, features = queries.shape[2:]
    heads = cross_bias.shape[0]
    width = features // heads
    blocks = lax.axis_size("seq")
    devices = lax.axis_size("chan") * blocks
    copies = devices // heads
    seats, lanes = stages(devices)
    place = lax.axis_index("chan") * blocks + lax.axis_index("seq")
    places = place.astype(jnp.int32)[None]
    kind = queries.dtype
    vmem = pl.BlockSpec(memory_space=pltpu.VMEM)
    smem = pl.BlockSpec(memory_space=pltpu.SMEM)
    anywhere = pl.BlockSpec(memory_space=pl.ANY)

    def layout(per_a, per_b):
        shapes = [jax.ShapeDtypeStruct((len(seats),) + per_a, kind)] * len(lanes)
        return shapes + [jax.ShapeDtypeStruct((len(lanes),) + per_b, kind)] * len(seats)

    sends = layout((2, rows, width), (2, rows, width))
    packed = pl.pallas_call(
        functools.partial(pack_kernel, copies),
        out_shape=sends,
        in_specs=[smem] + [anywhere] * 4,
        out_specs=[vmem] * len(sends),
        scratch_shapes=[pltpu.SemaphoreType.DMA((devices, 4))],
        compiler_params=pltpu.CompilerParams(vmem_limit_bytes=PACK_BYTES),
        name="pack",
    )(places, queries[0, 0], keys[0, 0], values[0, 0], out_grad[0, 0])
    first_a, last_a, first_b, last_b = exchanged(packed[: len(lanes)], packed[len(lanes) :], seats, lanes)

    half = rows // 2
    both = 2 * rows
    tiles = min(LOOKBACK + 1, blocks)
    pay_a, pay_b = 3 * half + EXTRA, 3 * half
    backs = layout((pay_a, width), (pay_b, width))
    arrived = first_a + last_a + first_b + last_b
    back = pl.pallas_call(
        functools.partial(head_kernel, copies),
        out_shape=backs,
        in_specs=[smem, smem, smem] + [anywhere] * len(arrived),
        out_specs=[anywhere] * len(backs),
        scratch_shapes=[
            pltpu.VMEM((devices, 2, rows, width), kind),
            pltpu.VMEM((devices, 2, rows, width), kind),
            pltpu.VMEM((devices, pay_a, width), kind),
            pltpu.VMEM((devices, pay_b, width), kind),
            pltpu.VMEM((blocks, width, both), kind),
            pltpu.VMEM((tiles, both, both), jnp.float32),
            pltpu.VMEM((tiles, both, both), jnp.float32),
            pltpu.VMEM((blocks, both, width), jnp.float32),
            pltpu.VMEM((blocks, both, width), jnp.float32),
            pltpu.VMEM((8, rows), jnp.float32),
            pltpu.SemaphoreType.DMA((devices, 2)),
            pltpu.SemaphoreType.DMA((devices, 2)),
        ],
        compiler_params=pltpu.CompilerParams(vmem_limit_bytes=HEAD_BYTES),
        name="head",
    )(lengths, places, cross_bias, *arrived)
    first_a, last_a, first_b, last_b = exchanged(back[: len(lanes)], back[len(lanes) :], seats, lanes)

    pieces = jnp.stack(
        [
            (first_a[i][0] if j == 0 else last_a[j - 1][i])[3 * half, :3].astype(jnp.float32)
            for i in range(len(lanes))
            for j in range(len(seats))
        ]
    )
    masks = jnp.array([lane + seat for lane in lanes for seat in seats], jnp.int32)
    chosen = (masks ^ place)[None] // copies == jnp.arange(heads, dtype=jnp.int32)[:, None]
    sums = pieces[:, 0] + pieces[:, 1] + pieces[:, 2]
    bias_out = summed_over(jnp.sum(jnp.where(chosen, sums[None], 0.0), axis=1), "dp")

    flat = jax.ShapeDtypeStruct((rows, features), kind)
    arrived = first_a + last_a + first_b + last_b
    grads = pl.pallas_call(
        functools.partial(unpack_kernel, copies),
        out_shape=(flat, flat, flat),
        in_specs=[smem] + [anywhere] * len(arrived),
        out_specs=(vmem, vmem, vmem),
        scratch_shapes=[
            pltpu.VMEM((devices, pay_a, width), kind),
            pltpu.VMEM((devices, pay_b, width), kind),
            pltpu.SemaphoreType.DMA((devices, 2)),
        ],
        compiler_params=pltpu.CompilerParams(vmem_limit_bytes=PACK_BYTES),
        name="unpack",
    )(places, *arrived)
    return tuple(grad[None, None] for grad in grads) + (bias_out,)


def solution(mesh):
    placed = P("dp", "chan", "seq", None)
    return jax.shard_map(
        shards,
        mesh=mesh,
        in_specs=(placed, placed, placed, placed, P(), P("dp")),
        out_specs=(placed, placed, placed, P()),
        check_vma=False,
    )
```

```python
import functools
import math

import jax
import jax.numpy as jnp
from jax import lax
from jax.experimental import pallas as pl
from jax.experimental.pallas import tpu as pltpu
from jax.sharding import PartitionSpec as P


LOOKBACK = 6
NEG_FILL = -1e30
EXTRA = 8
PACK_BYTES = 8 << 20
HEAD_BYTES = 20 << 20


def stages(devices):
    seats = [0, 1, devices // 2, devices // 2 + 1]
    lanes = [2 * step for step in range(devices // 4)]
    return seats, lanes


def run_all(copies):
    for copy in copies:
        copy.start()
    for copy in copies:
        copy.wait()


def pack_kernel(copies, by_lane, place_ref, first_ref, second_ref, *refs):
    sems = refs[-1]
    seats, lanes = stages(sems.shape[0])
    width = refs[0].shape[-1]
    started = []
    for i, lane in enumerate(lanes):
        for j, seat in enumerate(seats):
            head = (place_ref[0] ^ (lane + seat)) // copies
            columns = pl.ds(pl.multiple_of(head * width, width), width)
            target = refs[i].at[j] if by_lane else refs[j].at[i]
            for kind, source in enumerate((first_ref, second_ref)):
                started.append(
                    pltpu.make_async_copy(source.at[:, columns], target.at[kind], sems.at[len(seats) * i + j, kind])
                )
    run_all(started)


def unpack_kernel(copies, part, place_ref, *refs):
    sems, home, sums = refs[-1], refs[-2], refs[-3]
    outs = refs[-6:-3]
    pieces = refs[:-6] if part == 0 else refs[:-9]
    devices = sems.shape[0]
    seats, lanes = stages(devices)
    width = home.shape[2]
    half = outs[0].shape[0] // 2
    window = pl.ds(part * half, half)
    started = []
    for i, lane in enumerate(lanes):
        for j, seat in enumerate(seats):
            source = piece(pieces, part, i, j, seats, lanes)
            other = place_ref[0] ^ (lane + seat)
            if copies > 1:
                started.append(pltpu.make_async_copy(source, home.at[other], sems.at[len(seats) * i + j, 0]))
                continue
            columns = pl.ds(pl.multiple_of(other * width, width), width)
            for kind, out in enumerate(outs):
                rows = source.at[pl.ds(kind * half, half)]
                started.append(pltpu.make_async_copy(rows, out.at[window, columns], sems.at[len(seats) * i + j, kind]))
    run_all(started)
    if copies > 1:
        for head in range(devices // copies):
            columns = pl.ds(head * width, width)
            for kind, out in enumerate(outs):
                rows = pl.ds(kind * half, half)
                value = home[head * copies, rows].astype(jnp.float32)
                for other in range(1, copies):
                    value = value + home[head * copies + other, rows].astype(jnp.float32)
                sums[kind, :, columns] = value.astype(sums.dtype)
        run_all([pltpu.make_async_copy(sums.at[kind], out.at[window], sems.at[0, kind]) for kind, out in enumerate(outs)])


def piece(pieces, part, i, j, seats, lanes):
    firsts = len(seats) if part else len(lanes)
    near, far = (j, i) if part else (i, j)
    return pieces[near].at[0] if far == 0 else pieces[firsts + far - 1].at[near]


def gathered(place, refs, targets, sems, seats, lanes):
    cut = len(lanes) + len(seats) - 1
    started = []
    for i, lane in enumerate(lanes):
        for j, seat in enumerate(seats):
            other = place ^ (lane + seat)
            for part in range(2):
                source = piece(refs[part * cut : (part + 1) * cut], part, i, j, seats, lanes)
                started.append(pltpu.make_async_copy(source, targets[part].at[other], sems.at[len(seats) * i + j, part]))
    return started


def head_kernel(copies, length_ref, place_ref, bias_ref, *refs):
    got_sems, send_sems = refs[-2], refs[-1]
    qk_ref, vg_ref, out_a, out_b, kt_ref, s_ref, d_ref, dk_ref, dv_ref, bias_acc = refs[-12:-2]
    devices, _, rows, width = qk_ref.shape
    seats, lanes = stages(devices)
    arrays = refs[:-12]
    inputs = arrays[: 2 * (len(seats) + len(lanes) - 1)]
    outputs = arrays[len(inputs) :]
    place = place_ref[0]
    arriving = gathered(place, inputs, (qk_ref, vg_ref), got_sems, seats, lanes)
    blocks = devices // 2
    half = rows // 2
    both = 2 * rows
    root_scale = 1.0 / math.sqrt(width)
    log2_scale = root_scale * math.log2(math.e)
    length = length_ref[0]
    bias = bias_ref[place // copies] * math.log2(math.e)
    part = place % copies

    def pair(kind, block):
        source, kind = (qk_ref, kind) if kind < 2 else (vg_ref, kind - 2)
        return jnp.concatenate([source[block, kind], source[blocks + block, kind]], axis=0)

    def put(kind, c, block, tile):
        out_a[c * blocks + block, kind * half : (kind + 1) * half] = tile[:half]
        out_b[c * blocks + block, kind * half : (kind + 1) * half] = tile[half:]

    def dot(left, right, contract):
        return lax.dot_general(left, right, (contract, ((), ())), preferred_element_type=jnp.float32)

    column = lax.broadcasted_iota(jnp.int32, (1, both), 1)
    own = [jnp.where((column // rows) == c, 0.0, bias) for c in range(2)]
    key_row = lax.broadcasted_iota(jnp.int32, (rows, both), 0)
    query_column = lax.broadcasted_iota(jnp.int32, (rows, both), 1) % rows
    causal = key_row <= query_column
    in_reach = key_row > query_column

    for copy in arriving:
        copy.start()
    out_a[...] = jnp.zeros_like(out_a)
    out_b[...] = jnp.zeros_like(out_b)
    dk_ref[...] = jnp.zeros_like(dk_ref)
    dv_ref[...] = jnp.zeros_like(dv_ref)
    bias_acc[...] = jnp.zeros_like(bias_acc)

    def fold(tile, op):
        return op(tile.reshape(tile.shape[0] // 8, 8, tile.shape[1]), axis=0)

    def row_block(block, tiles):
        queries = pair(0, block)
        grads = pair(3, block)
        first = block - (tiles - 1)
        peak = jnp.full((8, both), NEG_FILL, jnp.float32)
        for t in range(tiles):
            raw = dot(pair(1, first + t), queries, ((1,), (1,)))
            for c in range(2):
                tile = raw[c * rows : (c + 1) * rows] * log2_scale + own[c]
                if t == tiles - 1:
                    tile = jnp.where(causal, tile, NEG_FILL)
                if tiles == LOOKBACK + 1 and t == 0:
                    tile = jnp.where(in_reach, tile, NEG_FILL)
                s_ref[t, c * rows : (c + 1) * rows] = tile
                peak = jnp.maximum(peak, fold(tile, jnp.max))
        peak = jnp.max(peak, axis=0, keepdims=True)
        total = jnp.zeros((8, both), jnp.float32)
        moment = jnp.zeros((8, both), jnp.float32)
        for t in range(tiles):
            weight_grad = dot(pair(2, first + t), grads, ((1,), (1,)))
            d_ref[t] = weight_grad
            power = jnp.exp2(s_ref[t] - peak)
            s_ref[t] = power
            total = total + fold(power, jnp.sum)
            moment = moment + fold(power * weight_grad, jnp.sum)
        total = jnp.sum(total, axis=0, keepdims=True)
        moment = jnp.sum(moment, axis=0, keepdims=True)
        frame = block * rows + column % rows
        live = frame < length
        if copies > 1:
            live = live & ((column * copies) // both == part)
        inverse = jnp.where(live, 1.0 / total, 0.0)
        delta = moment * inverse
        query_sum = jnp.zeros((width, both), jnp.float32)
        cross = jnp.zeros((8, rows), jnp.float32)
        for t in range(tiles):
            weights = s_ref[t] * inverse
            score_grad = weights * (d_ref[t] - delta)
            cross = cross + fold(score_grad[:rows, rows:], jnp.sum) + fold(score_grad[rows:, :rows], jnp.sum)
            weight_low = weights.astype(jnp.bfloat16)
            score_low = score_grad.astype(jnp.bfloat16)
            dv_ref[first + t] += dot(weight_low, grads, ((1,), (0,)))
            dk_ref[first + t] += dot(score_low, queries, ((1,), (0,)))
            query_sum = query_sum + dot(kt_ref[first + t], score_low, ((1,), (0,)))
        bias_acc[...] += cross
        query_grad = (query_sum.T * root_scale).astype(jnp.bfloat16)
        put(0, 0, block, query_grad[:rows])
        put(0, 1, block, query_grad[rows:])

    for copy in arriving:
        copy.wait()
    for block in range(blocks):
        kt_ref[block] = pair(1, block).T

    live_blocks = jnp.minimum((length + rows - 1) // rows, blocks)
    for block in range(min(LOOKBACK, blocks)):
        @pl.when(block < live_blocks)
        def _():
            row_block(block, block + 1)

    if blocks > LOOKBACK:
        def step(block, carried):
            row_block(block, LOOKBACK + 1)
            return carried

        lax.fori_loop(LOOKBACK, live_blocks, step, 0)

    for block in range(blocks):
        key_grad = (dk_ref[block] * root_scale).astype(jnp.bfloat16)
        value_grad = dv_ref[block].astype(jnp.bfloat16)
        for c in range(2):
            put(1, c, block, key_grad[c * rows : (c + 1) * rows])
            put(2, c, block, value_grad[c * rows : (c + 1) * rows])

    whole = jnp.sum(jnp.sum(bias_acc[...], axis=0, keepdims=True), axis=1, keepdims=True)
    whole = jnp.broadcast_to(whole, (1, width))
    high = whole.astype(jnp.bfloat16)
    rest = whole - high.astype(jnp.float32)
    middle = rest.astype(jnp.bfloat16)
    low = (rest - middle.astype(jnp.float32)).astype(jnp.bfloat16)
    lane = lax.broadcasted_iota(jnp.int32, (1, width), 1)
    pieces = jnp.where(
        lane == 0,
        high.astype(jnp.float32),
        jnp.where(lane == 1, middle.astype(jnp.float32), jnp.where(lane == 2, low.astype(jnp.float32), 0.0)),
    ).astype(jnp.bfloat16)
    pieces = jnp.broadcast_to(pieces, (EXTRA, width))
    for dest in range(devices):
        out_a[dest, 3 * half : 3 * half + EXTRA] = pieces
    leaving = []
    for i, lane in enumerate(lanes):
        for j, seat in enumerate(seats):
            other = place ^ (lane + seat)
            index = len(seats) * i + j
            leaving.append(pltpu.make_async_copy(out_a.at[other], outputs[i].at[j], send_sems.at[index, 0]))
            leaving.append(pltpu.make_async_copy(out_b.at[other], outputs[len(lanes) + j].at[i], send_sems.at[index, 1]))
    run_all(leaving)


def summed_over(value, axis):
    count = lax.axis_size(axis)
    if count & (count - 1):
        return lax.psum(value, axis)
    step = 1
    while step < count:
        pairs = [(source, source ^ step) for source in range(count)]
        value = value + lax.ppermute(value, axis, pairs)
        step *= 2
    return value


def in_hbm(value):
    return pltpu.with_memory_space_constraint(value, pltpu.HBM)


def moved(value, mask):
    devices = lax.axis_size("chan") * lax.axis_size("seq")
    return lax.ppermute(value, ("chan", "seq"), [(source, source ^ mask) for source in range(devices)])


def exchanged(by_lane, by_seat, seats, lanes):
    first_a = [by_lane[0]] + [moved(by_lane[i], lanes[i]) for i in range(1, len(lanes))]
    first_b = [by_seat[0]] + [moved(by_seat[j], seats[j]) for j in range(1, len(seats))]
    last_b = []
    for i in range(1, len(lanes)):
        waiting, first_a[i] = lax.optimization_barrier((jnp.stack([value[i] for value in first_b]), first_a[i]))
        last_b.append(moved(waiting, lanes[i]))
    last_a = [moved(jnp.stack([value[j] for value in first_a]), seats[j]) for j in range(1, len(seats))]
    return first_a + last_a, first_b + last_b


def layer(queries, keys, values, out_grad, cross_bias, lengths):
    rows, features = queries.shape[2:]
    heads = cross_bias.shape[0]
    width = features // heads
    blocks = lax.axis_size("seq")
    devices = lax.axis_size("chan") * blocks
    copies = devices // heads
    seats, lanes = stages(devices)
    place = lax.axis_index("chan") * blocks + lax.axis_index("seq")
    places = place.astype(jnp.int32)[None]
    kind = queries.dtype
    vmem = pl.BlockSpec(memory_space=pltpu.VMEM)
    smem = pl.BlockSpec(memory_space=pltpu.SMEM)
    anywhere = pl.BlockSpec(memory_space=pl.ANY)

    hbm = pl.BlockSpec(memory_space=pltpu.HBM)

    def shapes_a(*block):
        return [jax.ShapeDtypeStruct((len(seats),) + block, kind)] * len(lanes)

    def shapes_b(*block):
        return [jax.ShapeDtypeStruct((len(lanes),) + block, kind)] * len(seats)

    def pack(by_lane, first, second):
        sends = (shapes_a if by_lane else shapes_b)(2, rows, width)
        return pl.pallas_call(
            functools.partial(pack_kernel, copies, by_lane),
            out_shape=sends,
            in_specs=[smem, hbm, hbm],
            out_specs=[vmem] * len(sends),
            scratch_shapes=[pltpu.SemaphoreType.DMA((devices, 2))],
            compiler_params=pltpu.CompilerParams(vmem_limit_bytes=PACK_BYTES),
            name="pack_a" if by_lane else "pack_b",
        )(places, in_hbm(first[0, 0]), in_hbm(second[0, 0]))

    sent_a = pack(True, queries, keys)
    values, out_grad, sent_a = lax.optimization_barrier((values, out_grad, sent_a))
    sent_b = pack(False, values, out_grad)
    arrived_a, arrived_b = exchanged(sent_a, sent_b, seats, lanes)

    half = rows // 2
    both = 2 * rows
    tiles = min(LOOKBACK + 1, blocks)
    pay_a, pay_b = 3 * half + EXTRA, 3 * half
    backs = shapes_a(pay_a, width) + shapes_b(pay_b, width)
    arrived = arrived_a + arrived_b
    back = pl.pallas_call(
        functools.partial(head_kernel, copies),
        out_shape=backs,
        in_specs=[smem, smem, smem] + [anywhere] * len(arrived),
        out_specs=[anywhere] * len(backs),
        scratch_shapes=[
            pltpu.VMEM((devices, 2, rows, width), kind),
            pltpu.VMEM((devices, 2, rows, width), kind),
            pltpu.VMEM((devices, pay_a, width), kind),
            pltpu.VMEM((devices, pay_b, width), kind),
            pltpu.VMEM((blocks, width, both), kind),
            pltpu.VMEM((tiles, both, both), jnp.float32),
            pltpu.VMEM((tiles, both, both), jnp.float32),
            pltpu.VMEM((blocks, both, width), jnp.float32),
            pltpu.VMEM((blocks, both, width), jnp.float32),
            pltpu.VMEM((8, rows), jnp.float32),
            pltpu.SemaphoreType.DMA((devices, 2)),
            pltpu.SemaphoreType.DMA((devices, 2)),
        ],
        compiler_params=pltpu.CompilerParams(vmem_limit_bytes=HEAD_BYTES),
        name="head",
    )(lengths, places, cross_bias, *arrived)
    arrived_a, arrived_b = exchanged(back[: len(lanes)], back[len(lanes) :], seats, lanes)

    pieces = [
        (arrived_a[i][0] if j == 0 else arrived_a[len(lanes) + j - 1][i])[3 * half]
        for i in range(len(lanes))
        for j in range(len(seats))
    ]
    masks = jnp.array([lane + seat for lane in lanes for seat in seats], jnp.int32)
    chosen = (masks ^ place)[None] // copies == jnp.arange(heads, dtype=jnp.int32)[:, None]
    sums = jnp.sum(jnp.stack(pieces).astype(jnp.float32), axis=1)
    bias_out = summed_over(jnp.sum(jnp.where(chosen, sums[None], 0.0), axis=1), "dp")

    def unpack(part, arrived, earlier):
        flat = jax.ShapeDtypeStruct((rows, features), kind)
        stays = copies == 1
        return pl.pallas_call(
            functools.partial(unpack_kernel, copies, part),
            out_shape=(flat, flat, flat),
            in_specs=[smem] + [anywhere] * len(arrived) + [hbm] * len(earlier),
            out_specs=(hbm, hbm, hbm),
            scratch_shapes=[
                pltpu.VMEM((8, 8, 128) if stays else (3, half, features), kind),
                pltpu.VMEM((1, 8, width) if stays else (devices, pay_b if part else pay_a, width), kind),
                pltpu.SemaphoreType.DMA((devices, 3)),
            ],
            input_output_aliases={1 + len(arrived) + i: i for i in range(len(earlier))},
            compiler_params=pltpu.CompilerParams(vmem_limit_bytes=PACK_BYTES),
            name="unpack_b" if part else "unpack_a",
        )(places, *arrived, *earlier)

    grads = unpack(1, arrived_b, unpack(0, arrived_a, ()))
    return tuple(grad[None, None] for grad in grads) + (bias_out,)


def solution(mesh):
    placed = P("dp", "chan", "seq", None)
    return jax.shard_map(
        layer,
        mesh=mesh,
        in_specs=(placed, placed, placed, placed, P(), P("dp")),
        out_specs=(placed, placed, placed, P()),
        check_vma=False,
    )
```

```python
import functools
import math

import jax
import jax.numpy as jnp
from jax import lax
from jax.experimental import pallas as pl
from jax.experimental.pallas import tpu as pltpu
from jax.sharding import PartitionSpec as P


LOOKBACK = 6
NEG_FILL = -1e30
EXTRA = 8
LOG2_E = math.log2(math.e)
SLACK_BYTES = 6 << 20


def stages(devices):
    seats = [0, 1, devices // 2, devices // 2 + 1]
    lanes = [2 * step for step in range(devices // 4)]
    return seats, lanes


def places_of(devices):
    seats, lanes = stages(devices)
    return [(i, j, lane + seat) for i, lane in enumerate(lanes) for j, seat in enumerate(seats)]


def run_all(copies):
    for copy in copies:
        copy.start()
    for copy in copies:
        copy.wait()


def piece(pieces, lanes_first, i, j, devices):
    seats, lanes = stages(devices)
    firsts = len(lanes) if lanes_first else len(seats)
    near, far = (i, j) if lanes_first else (j, i)
    return pieces[near].at[0] if far == 0 else pieces[firsts + far - 1].at[near]


def gathered(place, pieces, lanes_first, target, sems):
    devices = target.shape[0]
    return [
        pltpu.make_async_copy(piece(pieces, lanes_first, i, j, devices), target.at[place ^ mask], sems.at[index])
        for index, (i, j, mask) in enumerate(places_of(devices))
    ]


def scattered(place, source, refs, lanes_first, sems):
    return [
        pltpu.make_async_copy(
            source.at[place ^ mask], (refs[i].at[j] if lanes_first else refs[j].at[i]), sems.at[index]
        )
        for index, (i, j, mask) in enumerate(places_of(source.shape[0]))
    ]


def pack_kernel(copies, lanes_first, place_ref, first_ref, second_ref, *refs):
    sems = refs[-1]
    width = refs[0].shape[-1]
    started = []
    for index, (i, j, mask) in enumerate(places_of(sems.shape[0])):
        head = (place_ref[0] ^ mask) // copies
        columns = pl.ds(pl.multiple_of(head * width, width), width)
        target = refs[i].at[j] if lanes_first else refs[j].at[i]
        for kind, source in enumerate((first_ref, second_ref)):
            started.append(pltpu.make_async_copy(source.at[:, columns], target.at[kind], sems.at[index, kind]))
    run_all(started)


def unpack_kernel(copies, lanes_first, place_ref, *refs):
    pieces, (out, sums, home, sems) = refs[:-4], refs[-4:]
    devices = sems.shape[0]
    rows = out.shape[0]
    width = home.shape[-1]
    started = []
    for index, (i, j, mask) in enumerate(places_of(devices)):
        other = place_ref[0] ^ mask
        source = piece(pieces, lanes_first, i, j, devices).at[pl.ds(0, rows)]
        target = home.at[other]
        if copies == 1:
            target = out.at[:, pl.ds(pl.multiple_of(other * width, width), width)]
        started.append(pltpu.make_async_copy(source, target, sems.at[index]))
    run_all(started)
    if copies > 1:
        for head in range(devices // copies):
            value = home[head * copies].astype(jnp.float32)
            for other in range(1, copies):
                value = value + home[head * copies + other].astype(jnp.float32)
            sums[:, head * width : (head + 1) * width] = value.astype(sums.dtype)
        run_all([pltpu.make_async_copy(sums, out, sems.at[0])])


def dot(left, right, contract):
    return lax.dot_general(left, right, (contract, ((), ())), preferred_element_type=jnp.float32)


def fold(tile, op):
    return op(tile.reshape(tile.shape[0] // 8, 8, tile.shape[1]), axis=0)


def pair(ref, kind, block):
    blocks = ref.shape[0] // 2
    return jnp.concatenate([ref[block, kind], ref[blocks + block, kind]], axis=0)


def tile_count(blocks):
    return sum(min(block, LOOKBACK) + 1 for block in range(blocks))


def for_blocks(length, rows, blocks, row_block):
    live_blocks = jnp.minimum((length + rows - 1) // rows, blocks)
    for block in range(min(LOOKBACK, blocks)):
        @pl.when(block < live_blocks)
        def _():
            row_block(block, tile_count(block), block + 1)

    if blocks > LOOKBACK:
        def step(block, carried):
            row_block(block, tile_count(LOOKBACK) + (block - LOOKBACK) * (LOOKBACK + 1), LOOKBACK + 1)
            return carried

        lax.fori_loop(LOOKBACK, live_blocks, step, 0)


def stats_kernel(copies, length_ref, place_ref, bias_ref, *refs):
    pieces, (qk_ref, weight_ref, sems) = refs[:-3], refs[-3:]
    devices, _, rows, width = qk_ref.shape
    both = 2 * rows
    log2_scale = LOG2_E / math.sqrt(width)
    place = place_ref[0]
    bias = bias_ref[place // copies] * LOG2_E
    part = place % copies
    length = length_ref[0]
    arriving = gathered(place, pieces, True, qk_ref, sems)
    run_all(arriving)

    column = lax.broadcasted_iota(jnp.int32, (1, both), 1)
    own = [jnp.where((column // rows) == c, 0.0, bias) for c in range(2)]
    key_row = lax.broadcasted_iota(jnp.int32, (rows, both), 0)
    query_column = lax.broadcasted_iota(jnp.int32, (rows, both), 1) % rows
    causal = key_row <= query_column
    in_reach = key_row > query_column

    def row_block(block, base, tiles):
        queries = pair(qk_ref, 0, block)
        first = block - (tiles - 1)
        peak = jnp.full((8, both), NEG_FILL, jnp.float32)
        for t in range(tiles):
            raw = dot(pair(qk_ref, 1, first + t), queries, ((1,), (1,)))
            for c in range(2):
                tile = raw[c * rows : (c + 1) * rows] * log2_scale + own[c]
                if t == tiles - 1:
                    tile = jnp.where(causal, tile, NEG_FILL)
                if tiles == LOOKBACK + 1 and t == 0:
                    tile = jnp.where(in_reach, tile, NEG_FILL)
                weight_ref[base + t, c * rows : (c + 1) * rows] = tile
                peak = jnp.maximum(peak, fold(tile, jnp.max))
        peak = jnp.max(peak, axis=0, keepdims=True)
        total = jnp.zeros((8, both), jnp.float32)
        for t in range(tiles):
            power = jnp.exp2(weight_ref[base + t] - peak)
            weight_ref[base + t] = power
            total = total + fold(power, jnp.sum)
        total = jnp.sum(total, axis=0, keepdims=True)
        live = block * rows + column % rows < length
        if copies > 1:
            live = live & ((column * copies) // both == part)
        inverse = jnp.where(live, 1.0 / total, 0.0)
        for t in range(tiles):
            weight_ref[base + t] = weight_ref[base + t] * inverse

    for_blocks(length, rows, devices // 2, row_block)


def values_kernel(length_ref, place_ref, weight_ref, *refs):
    arrays, (low_ref, sum_ref, got_sems, send_sems) = refs[:-4], refs[-4:]
    devices, rows, _ = low_ref.shape
    seats, lanes = stages(devices)
    blocks = devices // 2
    count = len(seats) + len(lanes) - 1
    vg_ref = arrays[count]
    place = place_ref[0]
    arriving = gathered(place, arrays[:count], False, vg_ref, got_sems)
    for copy in arriving:
        copy.start()
    sum_ref[...] = jnp.zeros_like(sum_ref)
    for copy in arriving:
        copy.wait()

    def row_block(block, base, tiles):
        grads = pair(vg_ref, 1, block)
        first = block - (tiles - 1)
        for t in range(tiles):
            sum_ref[first + t] += dot(weight_ref[base + t].astype(jnp.bfloat16), grads, ((1,), (0,)))

    for_blocks(length_ref[0], rows, blocks, row_block)
    for block in range(blocks):
        value_grad = sum_ref[block].astype(low_ref.dtype)
        low_ref[block] = value_grad[:rows]
        low_ref[blocks + block] = value_grad[rows:]
    run_all(scattered(place, low_ref, arrays[count + 1 :], True, send_sems))


def scores_kernel(length_ref, place_ref, qk_ref, vg_ref, weight_ref, *refs):
    outputs, (key_low, query_low, kt_ref, d_ref, dk_ref, bias_acc, key_sems, query_sems) = refs[:-8], refs[-8:]
    devices, _, rows, width = qk_ref.shape
    _, lanes = stages(devices)
    blocks = devices // 2
    both = 2 * rows
    root_scale = 1.0 / math.sqrt(width)
    place = place_ref[0]
    query_low[...] = jnp.zeros_like(query_low)
    dk_ref[...] = jnp.zeros_like(dk_ref)
    bias_acc[...] = jnp.zeros_like(bias_acc)
    for block in range(blocks):
        kt_ref[block] = pair(qk_ref, 1, block).T

    def row_block(block, base, tiles):
        queries = pair(qk_ref, 0, block)
        grads = pair(vg_ref, 1, block)
        first = block - (tiles - 1)
        delta = jnp.zeros((8, both), jnp.float32)
        for t in range(tiles):
            weight_grad = dot(pair(vg_ref, 0, first + t), grads, ((1,), (1,)))
            d_ref[t] = weight_grad
            delta = delta + fold(weight_ref[base + t] * weight_grad, jnp.sum)
        delta = jnp.sum(delta, axis=0, keepdims=True)
        query_sum = jnp.zeros((width, both), jnp.float32)
        cross = jnp.zeros((8, rows), jnp.float32)
        for t in range(tiles):
            score_grad = weight_ref[base + t] * (d_ref[t] - delta)
            cross = cross + fold(score_grad[:rows, rows:], jnp.sum) + fold(score_grad[rows:, :rows], jnp.sum)
            score_low = score_grad.astype(jnp.bfloat16)
            dk_ref[first + t] += dot(score_low, queries, ((1,), (0,)))
            query_sum = query_sum + dot(kt_ref[first + t], score_low, ((1,), (0,)))
        bias_acc[...] += cross
        query_grad = (query_sum.T * root_scale).astype(query_low.dtype)
        query_low[block] = query_grad[:rows]
        query_low[blocks + block] = query_grad[rows:]

    for_blocks(length_ref[0], rows, blocks, row_block)

    leaving = scattered(place, query_low, outputs[len(lanes) :], False, query_sems)
    for copy in leaving:
        copy.start()
    whole = jnp.sum(jnp.sum(bias_acc[...], axis=0, keepdims=True), axis=1, keepdims=True)
    whole = jnp.broadcast_to(whole, (1, width))
    high = whole.astype(jnp.bfloat16).astype(jnp.float32)
    middle = (whole - high).astype(jnp.bfloat16).astype(jnp.float32)
    low = (whole - high - middle).astype(jnp.bfloat16).astype(jnp.float32)
    lane = lax.broadcasted_iota(jnp.int32, (1, width), 1)
    pieces = jnp.where(lane == 0, high, jnp.where(lane == 1, middle, jnp.where(lane == 2, low, 0.0)))
    pieces = jnp.broadcast_to(pieces, (EXTRA, width)).astype(key_low.dtype)
    for block in range(blocks):
        key_grad = (dk_ref[block] * root_scale).astype(key_low.dtype)
        for c in range(2):
            key_low[c * blocks + block, :rows] = key_grad[c * rows : (c + 1) * rows]
            key_low[c * blocks + block, rows : rows + EXTRA] = pieces
    run_all(scattered(place, key_low, outputs[: len(lanes)], True, key_sems))
    for copy in leaving:
        copy.wait()


def summed_over(value, axis):
    count = lax.axis_size(axis)
    if count & (count - 1):
        return lax.psum(value, axis)
    step = 1
    while step < count:
        pairs = [(source, source ^ step) for source in range(count)]
        value = value + lax.ppermute(value, axis, pairs)
        step *= 2
    return value


def in_hbm(value):
    return pltpu.with_memory_space_constraint(value, pltpu.HBM)


def moved(value, mask):
    devices = lax.axis_size("chan") * lax.axis_size("seq")
    return lax.ppermute(value, ("chan", "seq"), [(source, source ^ mask) for source in range(devices)])


def both_after(value, earlier):
    return lax.optimization_barrier((value, earlier))


def over_lanes_first(by_lane, devices, earlier=None):
    _, lanes = stages(devices)
    first = [by_lane[0]]
    for i in range(1, len(lanes)):
        value = by_lane[i]
        if earlier is not None:
            value, earlier[i] = both_after(value, earlier[i])
        first.append(moved(value, lanes[i]))
    return first


def then_seats(first, devices):
    seats, _ = stages(devices)
    return [moved(jnp.stack([value[j] for value in first]), seats[j]) for j in range(1, len(seats))]


def over_seats_first(by_seat, devices, earlier):
    seats, lanes = stages(devices)
    first = [by_seat[0]] + [moved(by_seat[j], seats[j]) for j in range(1, len(seats))]
    last = []
    for i in range(1, len(lanes)):
        waiting, earlier[i] = both_after(jnp.stack([value[i] for value in first]), earlier[i])
        last.append(moved(waiting, lanes[i]))
    return first + last


def layer(queries, keys, values, out_grad, cross_bias, lengths):
    rows, features = queries.shape[2:]
    heads = cross_bias.shape[0]
    width = features // heads
    blocks = lax.axis_size("seq")
    devices = lax.axis_size("chan") * blocks
    copies = devices // heads
    seats, lanes = stages(devices)
    place = lax.axis_index("chan") * blocks + lax.axis_index("seq")
    places = place.astype(jnp.int32)[None]
    kind = queries.dtype
    both = 2 * rows
    tiles = min(LOOKBACK + 1, blocks)
    vmem = pl.BlockSpec(memory_space=pltpu.VMEM)
    smem = pl.BlockSpec(memory_space=pltpu.SMEM)
    anywhere = pl.BlockSpec(memory_space=pl.ANY)
    hbm = pl.BlockSpec(memory_space=pltpu.HBM)

    def by_lane(*block):
        return [jax.ShapeDtypeStruct((len(seats),) + block, kind)] * len(lanes)

    def by_seat(*block):
        return [jax.ShapeDtypeStruct((len(lanes),) + block, kind)] * len(seats)

    def size(*shapes):
        return sum(math.prod(shape.shape) * shape.dtype.itemsize for shape in shapes)

    def call(kernel, out_shape, in_specs, out_specs, scratch, grant, matmuls, args):
        flops = 2 * matmuls * tile_count(blocks) * both * both * width
        return pl.pallas_call(
            kernel,
            out_shape=out_shape,
            in_specs=in_specs,
            out_specs=out_specs,
            scratch_shapes=scratch,
            compiler_params=pltpu.CompilerParams(vmem_limit_bytes=grant + SLACK_BYTES),
            cost_estimate=pl.CostEstimate(flops=flops, bytes_accessed=2 << 20, transcendentals=0),
        )(*args)

    def pack(lanes_first, first, second):
        sends = by_lane(2, rows, width) if lanes_first else by_seat(2, rows, width)
        return call(
            functools.partial(pack_kernel, copies, lanes_first),
            sends,
            [smem, hbm, hbm],
            [vmem] * len(sends),
            [pltpu.SemaphoreType.DMA((devices, 2))],
            0,
            0,
            (places, in_hbm(first[0, 0]), in_hbm(second[0, 0])),
        )

    sent_a = pack(True, queries, keys)
    values, out_grad, sent_a = lax.optimization_barrier((values, out_grad, sent_a))
    sent_b = pack(False, values, out_grad)
    lane_a = over_lanes_first(sent_a, devices)
    arrived_b = over_seats_first(sent_b, devices, lane_a)
    arrived_a = lane_a + then_seats(lane_a, devices)

    gathered_shape = jax.ShapeDtypeStruct((devices, 2, rows, width), kind)
    weights_shape = jax.ShapeDtypeStruct((tile_count(blocks), both, both), jnp.float32)
    sums_shape = jax.ShapeDtypeStruct((blocks, both, width), jnp.float32)
    dma = pltpu.SemaphoreType.DMA((devices,))
    qk, weights = call(
        functools.partial(stats_kernel, copies),
        (gathered_shape, weights_shape),
        [smem, smem, smem] + [anywhere] * len(arrived_a),
        (vmem, vmem),
        [dma],
        size(gathered_shape, weights_shape),
        1,
        (lengths, places, cross_bias, *arrived_a),
    )
    sends = by_lane(rows, width)
    vg, *sent_v = call(
        values_kernel,
        [gathered_shape] + sends,
        [smem, smem, vmem] + [anywhere] * len(arrived_b),
        [vmem] + [anywhere] * len(sends),
        [
            pltpu.VMEM((devices, rows, width), kind),
            pltpu.VMEM(sums_shape.shape, jnp.float32),
            dma,
            dma,
        ],
        size(gathered_shape, weights_shape, sums_shape, gathered_shape),
        1,
        (lengths, places, weights, *arrived_b),
    )
    lane_v = over_lanes_first(sent_v, devices)
    sends = by_lane(rows + EXTRA, width) + by_seat(rows, width)
    sent = call(
        scores_kernel,
        sends,
        [smem, smem, vmem, vmem, vmem],
        [anywhere] * len(sends),
        [
            pltpu.VMEM((devices, rows + EXTRA, width), kind),
            pltpu.VMEM((devices, rows, width), kind),
            pltpu.VMEM((blocks, width, both), kind),
            pltpu.VMEM((tiles, both, both), jnp.float32),
            pltpu.VMEM(sums_shape.shape, jnp.float32),
            pltpu.VMEM((8, rows), jnp.float32),
            dma,
            dma,
        ],
        size(gathered_shape, gathered_shape, gathered_shape, gathered_shape, weights_shape, sums_shape),
        3,
        (lengths, places, qk, vg, weights),
    )
    lane_k = over_lanes_first(sent[: len(lanes)], devices, lane_v)
    arrived_q = over_seats_first(sent[len(lanes) :], devices, lane_k)
    arrived_v = lane_v + then_seats(lane_v, devices)
    arrived_k = lane_k + then_seats(lane_k, devices)

    pieces = [
        (arrived_k[i][0] if j == 0 else arrived_k[len(lanes) + j - 1][i])[rows] for i, j, _ in places_of(devices)
    ]
    masks = jnp.array([mask for _, _, mask in places_of(devices)], jnp.int32)
    chosen = (masks ^ place)[None] // copies == jnp.arange(heads, dtype=jnp.int32)[:, None]
    sums = jnp.sum(jnp.stack(pieces).astype(jnp.float32), axis=1)
    bias_out = summed_over(jnp.sum(jnp.where(chosen, sums[None], 0.0), axis=1), "dp")

    def unpack(lanes_first, arrived):
        sums_rows, homes = (16, 1) if copies == 1 else (rows, devices)
        return call(
            functools.partial(unpack_kernel, copies, lanes_first),
            jax.ShapeDtypeStruct((rows, features), kind),
            [smem] + [anywhere] * len(arrived),
            hbm,
            [
                pltpu.VMEM((sums_rows, features), kind),
                pltpu.VMEM((homes, rows, width), kind),
                dma,
            ],
            size(gathered_shape),
            0,
            (places, *arrived),
        )[None, None]

    value_out = unpack(True, arrived_v)
    key_out = unpack(True, arrived_k)
    query_out = unpack(False, arrived_q)
    return query_out, key_out, value_out, bias_out


def solution(mesh):
    placed = P("dp", "chan", "seq", None)
    return jax.shard_map(
        layer,
        mesh=mesh,
        in_specs=(placed, placed, placed, placed, P(), P("dp")),
        out_specs=(placed, placed, placed, P()),
        check_vma=False,
    )
```

```python
import functools
import math

import jax
import jax.numpy as jnp
from jax import lax
from jax.experimental import pallas as pl
from jax.experimental.pallas import tpu as pltpu
from jax.sharding import PartitionSpec as P


LOOKBACK = 6
NEG_FILL = -1e30
LOG2_E = math.log2(math.e)
SLACK_BYTES = 6 << 20


def stages(devices):
    seats = [0, 1, devices // 2, devices // 2 + 1]
    lanes = [2 * step for step in range(devices // 4)]
    return seats, lanes


def places_of(devices):
    seats, lanes = stages(devices)
    return [(i, j, lane + seat) for i, lane in enumerate(lanes) for j, seat in enumerate(seats)]


def run_all(copies):
    for copy in copies:
        copy.start()
    for copy in copies:
        copy.wait()


def piece(pieces, lanes_first, i, j, devices, kind=None):
    seats, lanes = stages(devices)
    firsts = len(lanes) if lanes_first else len(seats)
    near, far = (i, j) if lanes_first else (j, i)
    if far:
        return pieces[firsts + far - 1].at[near]
    return pieces[near].at[0] if kind is None else pieces[near].at[0, kind]


def gathered(place, pieces, lanes_first, target, sems, kind=None):
    devices = target.shape[0]
    return [
        pltpu.make_async_copy(piece(pieces, lanes_first, i, j, devices, kind), target.at[place ^ mask], sems.at[index])
        for index, (i, j, mask) in enumerate(places_of(devices))
    ]


def scattered(place, source, refs, lanes_first, sems):
    devices = source.shape[0]
    return [
        pltpu.make_async_copy(
            source.at[place ^ mask], (refs[i].at[j] if lanes_first else refs[j].at[i]), sems.at[index]
        )
        for index, (i, j, mask) in enumerate(places_of(devices))
    ]


def pack_kernel(copies, lanes_first, place_ref, first_ref, second_ref, *refs):
    sems = refs[-1]
    width = refs[0].shape[-1]
    started = []
    for index, (i, j, mask) in enumerate(places_of(sems.shape[0])):
        head = (place_ref[0] ^ mask) // copies
        columns = pl.ds(pl.multiple_of(head * width, width), width)
        target = refs[i].at[j] if lanes_first else refs[j].at[i]
        for kind, source in enumerate((first_ref, second_ref)):
            started.append(pltpu.make_async_copy(source.at[:, columns], target.at[kind], sems.at[index, kind]))
    run_all(started)


def unpack_kernel(copies, lanes_first, place_ref, *refs):
    pieces, (out, sums, home, sems) = refs[:-4], refs[-4:]
    devices = sems.shape[0]
    width = home.shape[-1]
    started = []
    for index, (i, j, mask) in enumerate(places_of(devices)):
        other = place_ref[0] ^ mask
        source = piece(pieces, lanes_first, i, j, devices)
        target = home.at[other]
        if copies == 1:
            target = out.at[:, pl.ds(pl.multiple_of(other * width, width), width)]
        started.append(pltpu.make_async_copy(source, target, sems.at[index]))
    run_all(started)
    if copies > 1:
        for head in range(devices // copies):
            value = home[head * copies].astype(jnp.float32)
            for other in range(1, copies):
                value = value + home[head * copies + other].astype(jnp.float32)
            sums[:, head * width : (head + 1) * width] = value.astype(sums.dtype)
        run_all([pltpu.make_async_copy(sums, out, sems.at[0])])


def dot(left, right, contract):
    return lax.dot_general(left, right, (contract, ((), ())), preferred_element_type=jnp.float32)


def fold(tile, op):
    return op(tile.reshape(tile.shape[0] // 8, 8, tile.shape[1]), axis=0)


def pair(ref, block, *kind):
    blocks = ref.shape[0] // 2
    return jnp.concatenate([ref[block, *kind], ref[blocks + block, *kind]], axis=0)


def tile_count(blocks):
    return sum(min(block, LOOKBACK) + 1 for block in range(blocks))


def for_blocks(length, rows, blocks, row_block):
    live_blocks = jnp.minimum((length + rows - 1) // rows, blocks)
    for block in range(min(LOOKBACK, blocks)):
        @pl.when(block < live_blocks)
        def _():
            row_block(block, tile_count(block), block + 1)

    if blocks > LOOKBACK:
        def step(block, carried):
            row_block(block, tile_count(LOOKBACK) + (block - LOOKBACK) * (LOOKBACK + 1), LOOKBACK + 1)
            return carried

        lax.fori_loop(LOOKBACK, live_blocks, step, 0)


def stats_kernel(copies, length_ref, place_ref, bias_ref, *refs):
    pieces, (qk_ref, weight_ref, sems) = refs[:-3], refs[-3:]
    devices, _, rows, width = qk_ref.shape
    both = 2 * rows
    log2_scale = LOG2_E / math.sqrt(width)
    place = place_ref[0]
    bias = bias_ref[place // copies] * LOG2_E
    part = place % copies
    length = length_ref[0]
    arriving = gathered(place, pieces, True, qk_ref, sems)
    run_all(arriving)

    column = lax.broadcasted_iota(jnp.int32, (1, both), 1)
    own = [jnp.where((column // rows) == c, 0.0, bias) for c in range(2)]
    key_row = lax.broadcasted_iota(jnp.int32, (rows, both), 0)
    query_column = lax.broadcasted_iota(jnp.int32, (rows, both), 1) % rows
    causal = key_row <= query_column
    in_reach = key_row > query_column

    def row_block(block, base, tiles):
        queries = pair(qk_ref, block, 0)
        first = block - (tiles - 1)
        peak = jnp.full((8, both), NEG_FILL, jnp.float32)
        for t in range(tiles):
            raw = dot(pair(qk_ref, first + t, 1), queries, ((1,), (1,)))
            for c in range(2):
                tile = raw[c * rows : (c + 1) * rows] * log2_scale + own[c]
                if t == tiles - 1:
                    tile = jnp.where(causal, tile, NEG_FILL)
                if tiles == LOOKBACK + 1 and t == 0:
                    tile = jnp.where(in_reach, tile, NEG_FILL)
                weight_ref[base + t, c * rows : (c + 1) * rows] = tile
                peak = jnp.maximum(peak, fold(tile, jnp.max))
        peak = jnp.max(peak, axis=0, keepdims=True)
        total = jnp.zeros((8, both), jnp.float32)
        for t in range(tiles):
            power = jnp.exp2(weight_ref[base + t] - peak)
            weight_ref[base + t] = power
            total = total + fold(power, jnp.sum)
        total = jnp.sum(total, axis=0, keepdims=True)
        live = block * rows + column % rows < length
        if copies > 1:
            live = live & ((column * copies) // both == part)
        inverse = jnp.where(live, 1.0 / total, 0.0)
        for t in range(tiles):
            weight_ref[base + t] = weight_ref[base + t] * inverse

    for_blocks(length, rows, devices // 2, row_block)


def values_kernel(length_ref, place_ref, weight_ref, *refs):
    arrays, (low_ref, sum_ref, got_sems, send_sems) = refs[:-4], refs[-4:]
    devices, rows, _ = low_ref.shape
    seats, lanes = stages(devices)
    blocks = devices // 2
    count = len(seats) + len(lanes) - 1
    grad_ref = arrays[count]
    place = place_ref[0]
    arriving = gathered(place, arrays[:count], False, grad_ref, got_sems, 0)
    for copy in arriving:
        copy.start()
    sum_ref[...] = jnp.zeros_like(sum_ref)
    for copy in arriving:
        copy.wait()

    def row_block(block, base, tiles):
        grads = pair(grad_ref, block)
        first = block - (tiles - 1)
        for t in range(tiles):
            sum_ref[first + t] += dot(weight_ref[base + t].astype(jnp.bfloat16), grads, ((1,), (0,)))

    for_blocks(length_ref[0], rows, blocks, row_block)
    for block in range(blocks):
        value_grad = sum_ref[block].astype(low_ref.dtype)
        low_ref[block] = value_grad[:rows]
        low_ref[blocks + block] = value_grad[rows:]
    run_all(scattered(place, low_ref, arrays[count + 1 :], True, send_sems))


def scores_kernel(copies, length_ref, place_ref, qk_ref, grad_ref, weight_ref, *refs):
    arrays, scratch = refs[:-9], refs[-9:]
    value_ref, low_ref, kt_ref, d_ref, dk_ref, bias_acc, got_sems, key_sems, query_sems = scratch
    devices, _, rows, width = qk_ref.shape
    seats, lanes = stages(devices)
    count = len(seats) + len(lanes) - 1
    blocks = devices // 2
    both = 2 * rows
    root_scale = 1.0 / math.sqrt(width)
    place = place_ref[0]
    arriving = gathered(place, arrays[:count], False, value_ref, got_sems, 1)
    bias_ref, outputs = arrays[count], arrays[count + 1 :]
    for copy in arriving:
        copy.start()
    low_ref[...] = jnp.zeros_like(low_ref)
    dk_ref[...] = jnp.zeros_like(dk_ref)
    bias_acc[...] = jnp.zeros_like(bias_acc)
    for block in range(blocks):
        kt_ref[block] = pair(qk_ref, block, 1).T
    for copy in arriving:
        copy.wait()

    def row_block(block, base, tiles):
        queries = pair(qk_ref, block, 0)
        grads = pair(grad_ref, block)
        first = block - (tiles - 1)
        delta = jnp.zeros((8, both), jnp.float32)
        for t in range(tiles):
            weight_grad = dot(pair(value_ref, first + t), grads, ((1,), (1,)))
            d_ref[t] = weight_grad
            delta = delta + fold(weight_ref[base + t] * weight_grad, jnp.sum)
        delta = jnp.sum(delta, axis=0, keepdims=True)
        query_sum = jnp.zeros((width, both), jnp.float32)
        cross = jnp.zeros((8, rows), jnp.float32)
        for t in range(tiles):
            score_grad = weight_ref[base + t] * (d_ref[t] - delta)
            cross = cross + fold(score_grad[:rows, rows:], jnp.sum) + fold(score_grad[rows:, :rows], jnp.sum)
            score_low = score_grad.astype(jnp.bfloat16)
            dk_ref[first + t] += dot(score_low, queries, ((1,), (0,)))
            query_sum = query_sum + dot(kt_ref[first + t], score_low, ((1,), (0,)))
        bias_acc[...] += cross
        query_grad = (query_sum.T * root_scale).astype(low_ref.dtype)
        low_ref[0, block] = query_grad[:rows]
        low_ref[0, blocks + block] = query_grad[rows:]

    for_blocks(length_ref[0], rows, blocks, row_block)

    leaving = scattered(place, low_ref.at[0], outputs[len(lanes) :], False, query_sems)
    for copy in leaving:
        copy.start()
    whole = jnp.sum(jnp.sum(bias_acc[...], axis=0, keepdims=True), axis=1, keepdims=True)
    lane = lax.broadcasted_iota(jnp.int32, bias_ref.shape, 1)
    bias_ref[...] = jnp.where(lane == place // copies, whole, 0.0)
    for block in range(blocks):
        key_grad = (dk_ref[block] * root_scale).astype(low_ref.dtype)
        for c in range(2):
            low_ref[1, c * blocks + block] = key_grad[c * rows : (c + 1) * rows]
    run_all(scattered(place, low_ref.at[1], outputs[: len(lanes)], True, key_sems))
    for copy in leaving:
        copy.wait()


def summed_over(value, axis):
    count = lax.axis_size(axis)
    if count & (count - 1):
        return lax.psum(value, axis)
    step = 1
    while step < count:
        pairs = [(source, source ^ step) for source in range(count)]
        value = value + lax.ppermute(value, axis, pairs)
        step *= 2
    return value


def in_hbm(value):
    return pltpu.with_memory_space_constraint(value, pltpu.HBM)


def moved(value, mask):
    devices = lax.axis_size("chan") * lax.axis_size("seq")
    return lax.ppermute(value, ("chan", "seq"), [(source, source ^ mask) for source in range(devices)])


def both_after(value, earlier):
    return lax.optimization_barrier((value, earlier))


def over_lanes_first(by_lane, devices, earlier=None):
    _, lanes = stages(devices)
    first = [by_lane[0]]
    for i in range(1, len(lanes)):
        value = by_lane[i]
        if earlier is not None:
            value, earlier[i] = both_after(value, earlier[i])
        first.append(moved(value, lanes[i]))
    return first


def then_seats(first, devices):
    seats, _ = stages(devices)
    return [moved(jnp.stack([value[j] for value in first]), seats[j]) for j in range(1, len(seats))]


def over_seats_first(by_seat, devices):
    seats, _ = stages(devices)
    return [by_seat[0]] + [moved(by_seat[j], seats[j]) for j in range(1, len(seats))]


def then_lanes(first, devices, earlier, free=None):
    _, lanes = stages(devices)
    last = []
    for i in range(1, len(lanes)):
        waiting = jnp.stack([value[i] for value in first])
        if i != free:
            waiting, earlier[i] = both_after(waiting, earlier[i])
        last.append(moved(waiting, lanes[i]))
    return last


def layer(queries, keys, values, out_grad, cross_bias, lengths):
    rows, features = queries.shape[2:]
    heads = cross_bias.shape[0]
    width = features // heads
    blocks = lax.axis_size("seq")
    devices = lax.axis_size("chan") * blocks
    copies = devices // heads
    seats, lanes = stages(devices)
    place = lax.axis_index("chan") * blocks + lax.axis_index("seq")
    places = place.astype(jnp.int32)[None]
    kind = queries.dtype
    both = 2 * rows
    tiles = min(LOOKBACK + 1, blocks)
    vmem = pl.BlockSpec(memory_space=pltpu.VMEM)
    smem = pl.BlockSpec(memory_space=pltpu.SMEM)
    anywhere = pl.BlockSpec(memory_space=pl.ANY)
    hbm = pl.BlockSpec(memory_space=pltpu.HBM)

    def by_lane(*block):
        return [jax.ShapeDtypeStruct((len(seats),) + block, kind)] * len(lanes)

    def by_seat(*block):
        return [jax.ShapeDtypeStruct((len(lanes),) + block, kind)] * len(seats)

    def size(*shapes):
        return sum(math.prod(shape.shape) * shape.dtype.itemsize for shape in shapes)

    def call(kernel, out_shape, in_specs, out_specs, scratch, grant, matmuls, args):
        flops = 2 * matmuls * tile_count(blocks) * both * both * width
        return pl.pallas_call(
            kernel,
            out_shape=out_shape,
            in_specs=in_specs,
            out_specs=out_specs,
            scratch_shapes=scratch,
            compiler_params=pltpu.CompilerParams(vmem_limit_bytes=grant + SLACK_BYTES),
            cost_estimate=pl.CostEstimate(flops=flops, bytes_accessed=2 << 20, transcendentals=0),
        )(*args)

    def pack(lanes_first, first, second):
        sends = by_lane(2, rows, width) if lanes_first else by_seat(2, rows, width)
        return call(
            functools.partial(pack_kernel, copies, lanes_first),
            sends,
            [smem, hbm, hbm],
            [vmem] * len(sends),
            [pltpu.SemaphoreType.DMA((devices, 2))],
            0,
            0,
            (places, in_hbm(first[0, 0]), in_hbm(second[0, 0])),
        )

    sent_a = pack(True, queries, keys)
    values, out_grad, sent_a = lax.optimization_barrier((values, out_grad, sent_a))
    sent_b = pack(False, out_grad, values)
    lane_a = over_lanes_first(sent_a, devices)
    seat_b = over_seats_first(sent_b, devices)
    lane_g = then_lanes([value[:, 0] for value in seat_b], devices, lane_a, len(lanes) - 1)
    gates = [None] + lane_g
    lane_w = then_lanes([value[:, 1] for value in seat_b], devices, gates)
    arrived_g, arrived_w = seat_b + gates[1:], seat_b + lane_w
    arrived_a = lane_a + then_seats(lane_a, devices)

    gathered_shape = jax.ShapeDtypeStruct((devices, 2, rows, width), kind)
    weights_shape = jax.ShapeDtypeStruct((tile_count(blocks), both, both), jnp.float32)
    sums_shape = jax.ShapeDtypeStruct((blocks, both, width), jnp.float32)
    dma = pltpu.SemaphoreType.DMA((devices,))
    qk, weights = call(
        functools.partial(stats_kernel, copies),
        (gathered_shape, weights_shape),
        [smem, smem, smem] + [anywhere] * len(arrived_a),
        (vmem, vmem),
        [dma],
        size(gathered_shape, weights_shape),
        1,
        (lengths, places, cross_bias, *arrived_a),
    )
    one_shape = jax.ShapeDtypeStruct((devices, rows, width), kind)
    sends = by_lane(rows, width)
    grads, *sent_v = call(
        values_kernel,
        [one_shape] + sends,
        [smem, smem, vmem] + [anywhere] * len(arrived_g),
        [vmem] + [anywhere] * len(sends),
        [
            pltpu.VMEM((devices, rows, width), kind),
            pltpu.VMEM(sums_shape.shape, jnp.float32),
            dma,
            dma,
        ],
        size(gathered_shape, weights_shape, sums_shape, gathered_shape),
        1,
        (lengths, places, weights, *arrived_g),
    )
    lane_v = over_lanes_first(sent_v, devices)
    sends = by_lane(rows, width) + by_seat(rows, width)
    bias_sum, *sent = call(
        functools.partial(scores_kernel, copies),
        [jax.ShapeDtypeStruct((1, heads), jnp.float32)] + sends,
        [smem, smem, vmem, vmem, vmem] + [anywhere] * len(arrived_w),
        [vmem] + [anywhere] * len(sends),
        [
            pltpu.VMEM(one_shape.shape, kind),
            pltpu.VMEM((2,) + one_shape.shape, kind),
            pltpu.VMEM((blocks, width, both), kind),
            pltpu.VMEM((tiles, both, both), jnp.float32),
            pltpu.VMEM(sums_shape.shape, jnp.float32),
            pltpu.VMEM((8, rows), jnp.float32),
            dma,
            dma,
            dma,
        ],
        size(gathered_shape, gathered_shape, gathered_shape, gathered_shape, weights_shape, sums_shape),
        3,
        (lengths, places, qk, grads, weights, *arrived_w),
    )
    lane_k = over_lanes_first(sent[: len(lanes)], devices, lane_v)
    seat_q = over_seats_first(sent[len(lanes) :], devices)
    arrived_q = seat_q + then_lanes(seat_q, devices, lane_k)
    arrived_v = lane_v + then_seats(lane_v, devices)
    arrived_k = lane_k + then_seats(lane_k, devices)

    bias_out = summed_over(bias_sum[0], "dp")
    mask = 1
    while mask < devices:
        bias_out = bias_out + moved(bias_out, mask)
        mask *= 2

    def unpack(lanes_first, arrived):
        sums_rows, homes = (16, 1) if copies == 1 else (rows, devices)
        return call(
            functools.partial(unpack_kernel, copies, lanes_first),
            jax.ShapeDtypeStruct((rows, features), kind),
            [smem] + [anywhere] * len(arrived),
            hbm,
            [
                pltpu.VMEM((sums_rows, features), kind),
                pltpu.VMEM((homes, rows, width), kind),
                dma,
            ],
            size(gathered_shape),
            0,
            (places, *arrived),
        )[None, None]

    value_out = unpack(True, arrived_v)
    key_out = unpack(True, arrived_k)
    query_out = unpack(False, arrived_q)
    return query_out, key_out, value_out, bias_out


def solution(mesh):
    placed = P("dp", "chan", "seq", None)
    return jax.shard_map(
        layer,
        mesh=mesh,
        in_specs=(placed, placed, placed, placed, P(), P("dp")),
        out_specs=(placed, placed, placed, P()),
        check_vma=False,
    )
```

```python
import functools
import math

import jax
import jax.numpy as jnp
from jax import lax
from jax.experimental import pallas as pl
from jax.experimental.pallas import tpu as pltpu
from jax.sharding import PartitionSpec as P


LOOKBACK = 6
NEG_FILL = -1e30
EXTRA = 8
LOG2_E = math.log2(math.e)
SLACK_BYTES = 6 << 20


def stages(devices):
    seats = [0, 1, devices // 2, devices // 2 + 1]
    lanes = [2 * step for step in range(devices // 4)]
    return seats, lanes


def places_of(devices):
    seats, lanes = stages(devices)
    return [(i, j, lane + seat) for i, lane in enumerate(lanes) for j, seat in enumerate(seats)]


def run_all(copies):
    for copy in copies:
        copy.start()
    for copy in copies:
        copy.wait()


def piece(pieces, lanes_first, i, j, devices):
    seats, lanes = stages(devices)
    firsts = len(lanes) if lanes_first else len(seats)
    near, far = (i, j) if lanes_first else (j, i)
    return pieces[firsts + far - 1].at[near] if far else pieces[near].at[0]


def gathered(place, pieces, lanes_first, target, sems):
    devices = target.shape[0]
    return [
        pltpu.make_async_copy(piece(pieces, lanes_first, i, j, devices), target.at[place ^ mask], sems.at[index])
        for index, (i, j, mask) in enumerate(places_of(devices))
    ]


def scattered(place, source, refs, lanes_first, sems):
    devices = source.shape[0]
    return [
        pltpu.make_async_copy(
            source.at[place ^ mask], (refs[i].at[j] if lanes_first else refs[j].at[i]), sems.at[index]
        )
        for index, (i, j, mask) in enumerate(places_of(devices))
    ]


def pack_kernel(copies, lanes_first, place_ref, first_ref, second_ref, *refs):
    sems = refs[-1]
    width = refs[0].shape[-1]
    started = []
    for index, (i, j, mask) in enumerate(places_of(sems.shape[0])):
        head = (place_ref[0] ^ mask) // copies
        columns = pl.ds(pl.multiple_of(head * width, width), width)
        target = refs[i].at[j] if lanes_first else refs[j].at[i]
        for kind, source in enumerate((first_ref, second_ref)):
            started.append(pltpu.make_async_copy(source.at[:, columns], target.at[kind], sems.at[index, kind]))
    run_all(started)


def unpack_kernel(copies, part, place_ref, *refs):
    sems, home, sums = refs[-1], refs[-2], refs[-3]
    outs = refs[-6:-3]
    pieces = refs[:-6] if part == 0 else refs[:-9]
    devices = sems.shape[0]
    width = home.shape[2]
    half = outs[0].shape[0] // 2
    window = pl.ds(part * half, half)
    started = []
    for index, (i, j, mask) in enumerate(places_of(devices)):
        source = piece(pieces, part == 0, i, j, devices)
        other = place_ref[0] ^ mask
        if copies > 1:
            started.append(pltpu.make_async_copy(source, home.at[other], sems.at[index, 0]))
            continue
        columns = pl.ds(pl.multiple_of(other * width, width), width)
        for kind, out in enumerate(outs):
            rows = source.at[pl.ds(kind * half, half)]
            started.append(pltpu.make_async_copy(rows, out.at[window, columns], sems.at[index, kind]))
    run_all(started)
    if copies > 1:
        for head in range(devices // copies):
            columns = pl.ds(head * width, width)
            for kind, out in enumerate(outs):
                rows = pl.ds(kind * half, half)
                value = home[head * copies, rows].astype(jnp.float32)
                for other in range(1, copies):
                    value = value + home[head * copies + other, rows].astype(jnp.float32)
                sums[kind, :, columns] = value.astype(sums.dtype)
        run_all([pltpu.make_async_copy(sums.at[kind], out.at[window], sems.at[0, kind]) for kind, out in enumerate(outs)])


def dot(left, right, contract):
    return lax.dot_general(left, right, (contract, ((), ())), preferred_element_type=jnp.float32)


def fold(tile, op):
    return op(tile.reshape(tile.shape[0] // 8, 8, tile.shape[1]), axis=0)


def pair(ref, block, *kind):
    blocks = ref.shape[0] // 2
    return jnp.concatenate([ref[block, *kind], ref[blocks + block, *kind]], axis=0)


def tile_count(blocks):
    return sum(min(block, LOOKBACK) + 1 for block in range(blocks))


def for_groups(length, rows, blocks, on_group, off_group=None):
    early = min(LOOKBACK, blocks)
    group = 2 if early % 2 == 0 and (blocks - early) % 2 == 0 else 1
    visited = ((length + group * rows - 1) // (group * rows)) * group
    visited = jnp.minimum(visited, blocks)
    for start in range(0, early, group):
        @pl.when(start < visited)
        def _():
            on_group([(block, tile_count(block), block + 1) for block in range(start, start + group)])

        if off_group is not None:
            pl.when(start >= visited)(lambda: off_group([start + k for k in range(group)]))
    if blocks > early:
        def member(block):
            return block, tile_count(LOOKBACK) + (block - LOOKBACK) * (LOOKBACK + 1), LOOKBACK + 1

        def live(step, carried):
            on_group([member(LOOKBACK + step * group + k) for k in range(group)])
            return carried

        def dead(step, carried):
            off_group([LOOKBACK + step * group + k for k in range(group)])
            return carried

        late = jnp.maximum(visited - LOOKBACK, 0) // group
        lax.fori_loop(0, late, live, 0)
        if off_group is not None:
            lax.fori_loop(late, (blocks - early) // group, dead, 0)
    return visited


def stats_kernel(copies, length_ref, place_ref, bias_ref, *refs):
    pieces, (qk_ref, kt_ref, power_ref, inverse_ref, sems) = refs[:-5], refs[-5:]
    devices, _, rows, width = qk_ref.shape
    blocks = devices // 2
    both = 2 * rows
    log2_scale = LOG2_E / math.sqrt(width)
    place = place_ref[0]
    bias = bias_ref[place // copies] * LOG2_E
    part = place % copies
    length = length_ref[0]
    run_all(gathered(place, pieces, True, qk_ref, sems))

    column = lax.broadcasted_iota(jnp.int32, (1, both), 1)
    own = [jnp.where((column // rows) == c, 0.0, bias) for c in range(2)]
    key_row = lax.broadcasted_iota(jnp.int32, (rows, both), 0)
    query_column = lax.broadcasted_iota(jnp.int32, (rows, both), 1) % rows
    for block in range(blocks):
        kt_ref[block] = pair(qk_ref, block, 1).T

    def on_group(members):
        shifts = []
        for block, base, tiles in members:
            queries = pair(qk_ref, block, 0)
            first = block - (tiles - 1)
            peaks = [jnp.full((8, both), NEG_FILL, jnp.float32)] * 2
            for t in range(tiles):
                raw = dot(pair(qk_ref, first + t, 1), queries, ((1,), (1,)))
                for c in range(2):
                    tile = raw[c * rows : (c + 1) * rows]
                    if t == tiles - 1:
                        tile = jnp.where(key_row <= query_column, tile, NEG_FILL)
                    if tiles == LOOKBACK + 1 and t == 0:
                        tile = jnp.where(key_row > query_column, tile, NEG_FILL)
                    power_ref[base + t, c * rows : (c + 1) * rows] = tile
                    peaks[c] = jnp.maximum(peaks[c], fold(tile, jnp.max))
            peaks = [jnp.max(peaks[c], axis=0, keepdims=True) * log2_scale + own[c] for c in range(2)]
            peak = jnp.maximum(peaks[0], peaks[1])
            shifts.append([own[c] - peak for c in range(2)])
        for (block, base, tiles), shift in zip(members, shifts):
            total = jnp.zeros((8, both), jnp.float32)
            for t in range(tiles):
                for c in range(2):
                    window = slice(c * rows, (c + 1) * rows)
                    power = jnp.exp2(power_ref[base + t, window] * log2_scale + shift[c])
                    power_ref[base + t, window] = power
                    total = total + fold(power, jnp.sum)
            total = jnp.sum(total, axis=0, keepdims=True)
            live = block * rows + column % rows < length
            if copies > 1:
                live = live & ((column * copies) // both == part)
            inverse_ref[block] = jnp.broadcast_to(jnp.where(live, 1.0 / total, 0.0), (8, both))

    for_groups(length, rows, blocks, on_group)


def grads_kernel(length_ref, place_ref, qk_ref, kt_ref, power_ref, inverse_ref, *refs):
    arrays, scratch = refs[:-9], refs[-9:]
    gv_ref, low_a, low_b, d_ref, dk_ref, dv_ref, bias_acc, got_sems, send_sems = scratch
    devices, _, rows, width = qk_ref.shape
    seats, lanes = stages(devices)
    count = len(seats) + len(lanes) - 1
    blocks = devices // 2
    both = 2 * rows
    half = rows // 2
    root_scale = 1.0 / math.sqrt(width)
    place = place_ref[0]
    outputs = arrays[count:]
    run_all(gathered(place, arrays[:count], False, gv_ref, got_sems))
    bias_acc[...] = jnp.zeros_like(bias_acc)

    def put(kind, c, block, tile):
        low_a[c * blocks + block, kind * half : (kind + 1) * half] = tile[:half]
        low_b[c * blocks + block, kind * half : (kind + 1) * half] = tile[half:]

    def on_group(members):
        deltas = []
        for k, (block, base, tiles) in enumerate(members):
            grads = pair(gv_ref, block, 0)
            first = block - (tiles - 1)
            moment = jnp.zeros((8, both), jnp.float32)
            for t in range(tiles):
                weight_grad = dot(pair(gv_ref, first + t, 1), grads, ((1,), (1,)))
                d_ref[k, t] = weight_grad
                moment = moment + fold(power_ref[base + t] * weight_grad, jnp.sum)
            deltas.append(jnp.sum(moment, axis=0, keepdims=True) * inverse_ref[block, :1])
        sums = []
        for k, (block, base, tiles) in enumerate(members):
            queries = pair(qk_ref, block, 0)
            grads = pair(gv_ref, block, 0)
            inverse = inverse_ref[block, :1]
            first = block - (tiles - 1)
            query_sum = jnp.zeros((width, both), jnp.float32)
            cross = jnp.zeros((8, rows), jnp.float32)
            for t in range(tiles):
                weights = power_ref[base + t] * inverse
                score_grad = weights * (d_ref[k, t] - deltas[k])
                cross = cross + fold(score_grad[:rows, rows:], jnp.sum) + fold(score_grad[rows:, :rows], jnp.sum)
                score_low = score_grad.astype(jnp.bfloat16)
                value_term = dot(weights.astype(jnp.bfloat16), grads, ((1,), (0,)))
                key_term = dot(score_low, queries, ((1,), (0,)))
                if t == tiles - 1:
                    dv_ref[block] = value_term
                    dk_ref[block] = key_term
                else:
                    dv_ref[first + t] += value_term
                    dk_ref[first + t] += key_term
                query_sum = query_sum + dot(kt_ref[first + t], score_low, ((1,), (0,)))
            bias_acc[...] += cross
            sums.append(query_sum)
        for (block, _, _), query_sum in zip(members, sums):
            query_grad = (query_sum * root_scale).T.astype(low_a.dtype)
            for c in range(2):
                put(0, c, block, query_grad[c * rows : (c + 1) * rows])

    def off_group(members):
        for block in members:
            for c in range(2):
                put(0, c, block, jnp.zeros((rows, width), low_a.dtype))

    visited = for_groups(length_ref[0], rows, blocks, on_group, off_group)

    whole = jnp.sum(jnp.sum(bias_acc[...], axis=0, keepdims=True), axis=1, keepdims=True)
    whole = jnp.broadcast_to(whole, (1, width))
    high = whole.astype(jnp.bfloat16).astype(jnp.float32)
    middle = (whole - high).astype(jnp.bfloat16).astype(jnp.float32)
    low = (whole - high - middle).astype(jnp.bfloat16).astype(jnp.float32)
    lane = lax.broadcasted_iota(jnp.int32, (1, width), 1)
    pieces = jnp.where(lane == 0, high, jnp.where(lane == 1, middle, jnp.where(lane == 2, low, 0.0)))
    pieces = jnp.broadcast_to(pieces, (EXTRA, width)).astype(low_a.dtype)
    for block in range(blocks):
        seen = block < visited
        key_grad = jnp.where(seen, dk_ref[block] * root_scale, 0.0).astype(low_a.dtype)
        value_grad = jnp.where(seen, dv_ref[block], 0.0).astype(low_a.dtype)
        for c in range(2):
            put(1, c, block, key_grad[c * rows : (c + 1) * rows])
            put(2, c, block, value_grad[c * rows : (c + 1) * rows])
            low_a[c * blocks + block, 3 * half : 3 * half + EXTRA] = pieces
    leaving = scattered(place, low_a, outputs[: len(lanes)], True, send_sems.at[0])
    leaving += scattered(place, low_b, outputs[len(lanes) :], False, send_sems.at[1])
    run_all(leaving)


def summed_over(value, axis):
    count = lax.axis_size(axis)
    if count & (count - 1):
        return lax.psum(value, axis)
    step = 1
    while step < count:
        pairs = [(source, source ^ step) for source in range(count)]
        value = value + lax.ppermute(value, axis, pairs)
        step *= 2
    return value


def in_hbm(value):
    return pltpu.with_memory_space_constraint(value, pltpu.HBM)


def moved(value, mask):
    devices = lax.axis_size("chan") * lax.axis_size("seq")
    return lax.ppermute(value, ("chan", "seq"), [(source, source ^ mask) for source in range(devices)])


def exchanged(by_lane, by_seat, devices):
    seats, lanes = stages(devices)
    first_a = [by_lane[0]] + [moved(by_lane[i], lanes[i]) for i in range(1, len(lanes))]
    first_b = [by_seat[0]] + [moved(by_seat[j], seats[j]) for j in range(1, len(seats))]
    last_b = []
    for i in range(1, len(lanes)):
        waiting, first_a[i] = lax.optimization_barrier((jnp.stack([value[i] for value in first_b]), first_a[i]))
        last_b.append(moved(waiting, lanes[i]))
    last_a = [moved(jnp.stack([value[j] for value in first_a]), seats[j]) for j in range(1, len(seats))]
    return first_a + last_a, first_b + last_b


def layer(queries, keys, values, out_grad, cross_bias, lengths):
    rows, features = queries.shape[2:]
    heads = cross_bias.shape[0]
    width = features // heads
    blocks = lax.axis_size("seq")
    devices = lax.axis_size("chan") * blocks
    copies = devices // heads
    seats, lanes = stages(devices)
    place = lax.axis_index("chan") * blocks + lax.axis_index("seq")
    places = place.astype(jnp.int32)[None]
    kind = queries.dtype
    both = 2 * rows
    tiles = min(LOOKBACK + 1, blocks)
    vmem = pl.BlockSpec(memory_space=pltpu.VMEM)
    smem = pl.BlockSpec(memory_space=pltpu.SMEM)
    anywhere = pl.BlockSpec(memory_space=pl.ANY)
    hbm = pl.BlockSpec(memory_space=pltpu.HBM)

    def by_lane(*block):
        return [jax.ShapeDtypeStruct((len(seats),) + block, kind)] * len(lanes)

    def by_seat(*block):
        return [jax.ShapeDtypeStruct((len(lanes),) + block, kind)] * len(seats)

    def size(*shapes):
        return sum(math.prod(shape.shape) * shape.dtype.itemsize for shape in shapes)

    def call(kernel, out_shape, in_specs, out_specs, scratch, grant, matmuls, args):
        flops = 2 * matmuls * tile_count(blocks) * both * both * width
        return pl.pallas_call(
            kernel,
            out_shape=out_shape,
            in_specs=in_specs,
            out_specs=out_specs,
            scratch_shapes=scratch,
            compiler_params=pltpu.CompilerParams(vmem_limit_bytes=grant + SLACK_BYTES),
            cost_estimate=pl.CostEstimate(flops=flops, bytes_accessed=2 << 20, transcendentals=0),
        )(*args)

    def pack(lanes_first, first, second):
        sends = by_lane(2, rows, width) if lanes_first else by_seat(2, rows, width)
        return call(
            functools.partial(pack_kernel, copies, lanes_first),
            sends,
            [smem, hbm, hbm],
            [vmem] * len(sends),
            [pltpu.SemaphoreType.DMA((devices, 2))],
            0,
            0,
            (places, in_hbm(first[0, 0]), in_hbm(second[0, 0])),
        )

    sent_a = pack(True, queries, keys)
    values, out_grad, sent_a = lax.optimization_barrier((values, out_grad, sent_a))
    sent_b = pack(False, out_grad, values)
    arrived_a, arrived_b = exchanged(sent_a, sent_b, devices)

    half = rows // 2
    group = 2
    two_shape = jax.ShapeDtypeStruct((devices, 2, rows, width), kind)
    turned_shape = jax.ShapeDtypeStruct((blocks, width, both), kind)
    power_shape = jax.ShapeDtypeStruct((tile_count(blocks), both, both), jnp.float32)
    inverse_shape = jax.ShapeDtypeStruct((blocks, 8, both), jnp.float32)
    sums_shape = jax.ShapeDtypeStruct((blocks, both, width), jnp.float32)
    low_a, low_b = (
        jax.ShapeDtypeStruct((devices, pay, width), kind) for pay in (3 * half + EXTRA, 3 * half)
    )
    d_shape = jax.ShapeDtypeStruct((group, tiles, both, both), jnp.float32)
    dma = pltpu.SemaphoreType.DMA((devices,))
    made = call(
        functools.partial(stats_kernel, copies),
        (two_shape, turned_shape, power_shape, inverse_shape),
        [smem, smem, smem] + [anywhere] * len(arrived_a),
        [vmem] * 4,
        [dma],
        size(two_shape, turned_shape, power_shape, inverse_shape),
        1,
        (lengths, places, cross_bias, *arrived_a),
    )
    sends = by_lane(*low_a.shape[1:]) + by_seat(*low_b.shape[1:])
    held = (two_shape, low_a, low_b, d_shape, sums_shape, sums_shape)
    back = call(
        grads_kernel,
        sends,
        [smem, smem] + [vmem] * 4 + [anywhere] * len(arrived_b),
        [anywhere] * len(sends),
        [pltpu.VMEM(shape.shape, shape.dtype) for shape in held]
        + [pltpu.VMEM((8, rows), jnp.float32), dma, pltpu.SemaphoreType.DMA((2, devices))],
        size(*held, two_shape, turned_shape, power_shape, inverse_shape),
        4,
        (lengths, places, *made, *arrived_b),
    )
    arrived_a, arrived_b = exchanged(back[: len(lanes)], back[len(lanes) :], devices)

    pieces = [
        (arrived_a[i][0] if j == 0 else arrived_a[len(lanes) + j - 1][i])[3 * half] for i, j, _ in places_of(devices)
    ]
    masks = jnp.array([mask for _, _, mask in places_of(devices)], jnp.int32)
    chosen = (masks ^ place)[None] // copies == jnp.arange(heads, dtype=jnp.int32)[:, None]
    sums = jnp.sum(jnp.stack(pieces).astype(jnp.float32), axis=1)
    bias_out = summed_over(jnp.sum(jnp.where(chosen, sums[None], 0.0), axis=1), "dp")

    def unpack(part, arrived, earlier):
        flat = jax.ShapeDtypeStruct((rows, features), kind)
        alone = copies == 1
        return pl.pallas_call(
            functools.partial(unpack_kernel, copies, part),
            out_shape=(flat, flat, flat),
            in_specs=[smem] + [anywhere] * len(arrived) + [hbm] * len(earlier),
            out_specs=(hbm, hbm, hbm),
            scratch_shapes=[
                pltpu.VMEM((8, 8, 128) if alone else (3, half, features), kind),
                pltpu.VMEM((1, 8, width) if alone else (devices,) + arrived[0].shape[1:], kind),
                pltpu.SemaphoreType.DMA((devices, 3)),
            ],
            input_output_aliases={1 + len(arrived) + i: i for i in range(len(earlier))},
            compiler_params=pltpu.CompilerParams(vmem_limit_bytes=SLACK_BYTES),
            name="unpack_b" if part else "unpack_a",
        )(places, *arrived, *earlier)

    grads = unpack(1, arrived_b, unpack(0, arrived_a, ()))
    return tuple(grad[None, None] for grad in grads) + (bias_out,)


def solution(mesh):
    placed = P("dp", "chan", "seq", None)
    return jax.shard_map(
        layer,
        mesh=mesh,
        in_specs=(placed, placed, placed, placed, P(), P("dp")),
        out_specs=(placed, placed, placed, P()),
        check_vma=False,
    )
```

```python
import functools
import math

import jax
import jax.numpy as jnp
from jax import lax
from jax.experimental import pallas as pl
from jax.experimental.pallas import tpu as pltpu
from jax.sharding import PartitionSpec as P


LOOKBACK = 6
NEG_FILL = -1e30
EXTRA = 8
LOG2_E = math.log2(math.e)
SLACK_BYTES = 6 << 20


def stages(devices):
    seats = [0, 1, devices // 2, devices // 2 + 1]
    lanes = [2 * step for step in range(devices // 4)]
    return seats, lanes


def places_of(devices):
    seats, lanes = stages(devices)
    return [(i, j, lane + seat) for i, lane in enumerate(lanes) for j, seat in enumerate(seats)]


def run_all(copies):
    for copy in copies:
        copy.start()
    for copy in copies:
        copy.wait()


def piece(pieces, lanes_first, i, j, devices):
    seats, lanes = stages(devices)
    firsts = len(lanes) if lanes_first else len(seats)
    near, far = (i, j) if lanes_first else (j, i)
    return pieces[firsts + far - 1].at[near] if far else pieces[near].at[0]


def position(place, other, blocks):
    mask = place ^ other
    return lax.rem(mask, blocks) // 2, lax.rem(mask, 2) + 2 * (mask // blocks)


def pack_kernel(copies, lanes_first, group, place_ref, first_ref, second_ref, *refs):
    sems = refs[-1]
    width = refs[0].shape[-1]
    started = []
    for index, (i, j, mask) in enumerate(places_of(sems.shape[0])):
        near, far = (i, j) if lanes_first else (j, i)
        if near not in group:
            continue
        head = (place_ref[0] ^ mask) // copies
        columns = pl.ds(pl.multiple_of(head * width, width), width)
        for kind, source in enumerate((first_ref, second_ref)):
            target = refs[group.index(near)].at[far, kind]
            started.append(pltpu.make_async_copy(source.at[:, columns], target, sems.at[index, kind]))
    run_all(started)


def unpack_kernel(copies, part, place_ref, *refs):
    sems, home, sums = refs[-1], refs[-2], refs[-3]
    outs = refs[-6:-3]
    pieces = refs[:-6] if part == 0 else refs[:-9]
    devices = sems.shape[0]
    width = home.shape[2]
    half = outs[0].shape[0] // 2
    window = pl.ds(part * half, half)
    started = []
    for index, (i, j, mask) in enumerate(places_of(devices)):
        source = piece(pieces, part == 0, i, j, devices)
        other = place_ref[0] ^ mask
        if copies > 1:
            started.append(pltpu.make_async_copy(source, home.at[other], sems.at[index, 0]))
            continue
        columns = pl.ds(pl.multiple_of(other * width, width), width)
        for kind, out in enumerate(outs):
            rows = source.at[pl.ds(kind * half, half)]
            started.append(pltpu.make_async_copy(rows, out.at[window, columns], sems.at[index, kind]))
    run_all(started)
    if copies > 1:
        for head in range(devices // copies):
            columns = pl.ds(head * width, width)
            for kind, out in enumerate(outs):
                rows = pl.ds(kind * half, half)
                value = home[head * copies, rows].astype(jnp.float32)
                for other in range(1, copies):
                    value = value + home[head * copies + other, rows].astype(jnp.float32)
                sums[kind, :, columns] = value.astype(sums.dtype)
        run_all([pltpu.make_async_copy(sums.at[kind], out.at[window], sems.at[0, kind]) for kind, out in enumerate(outs)])


def dot(left, right, contract):
    return lax.dot_general(left, right, (contract, ((), ())), preferred_element_type=jnp.float32)


def fold(tile, op):
    return op(tile.reshape(tile.shape[0] // 8, 8, tile.shape[1]), axis=0)


def pair(ref, place, block, kind, lanes_first):
    blocks = 2 * ref.shape[1 if not lanes_first else 0]
    parts = []
    for c in range(2):
        i, j = position(place, c * blocks + block, blocks)
        parts.append(ref[i, j, kind] if lanes_first else ref[j, i, kind])
    return jnp.concatenate(parts, axis=0)


def tile_count(blocks):
    return sum(min(block, LOOKBACK) + 1 for block in range(blocks))


def group_size(blocks):
    early = min(LOOKBACK, blocks)
    return 2 if early % 2 == 0 and (blocks - early) % 2 == 0 else 1


def for_groups(length, rows, blocks, on_group, off_group=None):
    early = min(LOOKBACK, blocks)
    group = group_size(blocks)
    visited = jnp.minimum(((length + group * rows - 1) // (group * rows)) * group, blocks)

    def either(members, higher):
        pl.when(members[0][0] < visited)(lambda: on_group(members, higher))
        if off_group is not None:
            pl.when(members[0][0] >= visited)(lambda: off_group(members, higher))

    def late(start, higher):
        members = [(start + k, tile_count(LOOKBACK) + (start + k - LOOKBACK) * (LOOKBACK + 1)) for k in range(group)]
        either([(block, base, LOOKBACK + 1) for block, base in members], higher)

    higher = None
    if blocks > early:
        late(blocks - group, None)

        def step(index, carried):
            start = blocks - (index + 1) * group
            late(start, [start + group + k for k in range(group)])
            return carried

        lax.fori_loop(1, (blocks - early) // group, step, 0)
        higher = [early + k for k in range(group)]
    for start in range(early - group, -1, -group):
        either([(block, tile_count(block), block + 1) for block in range(start, start + group)], higher)
        higher = [start + k for k in range(group)]


def stats_kernel(copies, length_ref, place_ref, bias_ref, qk_ref, kt_ref, power_ref, inverse_ref):
    rows, width = qk_ref.shape[3:]
    blocks = 2 * qk_ref.shape[1]
    both = 2 * rows
    log2_scale = LOG2_E / math.sqrt(width)
    place = place_ref[0]
    bias = bias_ref[place // copies] * LOG2_E
    part = place % copies
    length = length_ref[0]

    column = lax.broadcasted_iota(jnp.int32, (1, both), 1)
    own = [jnp.where((column // rows) == c, 0.0, bias) for c in range(2)]
    key_row = lax.broadcasted_iota(jnp.int32, (rows, both), 0)
    query_column = lax.broadcasted_iota(jnp.int32, (rows, both), 1) % rows
    for block in range(blocks):
        kt_ref[block] = pair(qk_ref, place, block, 1, False).T

    def on_group(members, higher):
        shifts = []
        for block, base, tiles in members:
            queries = pair(qk_ref, place, block, 0, False)
            first = block - (tiles - 1)
            peaks = [jnp.full((8, both), NEG_FILL, jnp.float32)] * 2
            for t in range(tiles):
                raw = dot(pair(qk_ref, place, first + t, 1, False), queries, ((1,), (1,)))
                for c in range(2):
                    tile = raw[c * rows : (c + 1) * rows]
                    if t == tiles - 1:
                        tile = jnp.where(key_row <= query_column, tile, NEG_FILL)
                    if tiles == LOOKBACK + 1 and t == 0:
                        tile = jnp.where(key_row > query_column, tile, NEG_FILL)
                    power_ref[base + t, c * rows : (c + 1) * rows] = tile
                    peaks[c] = jnp.maximum(peaks[c], fold(tile, jnp.max))
            peaks = [jnp.max(peaks[c], axis=0, keepdims=True) * log2_scale + own[c] for c in range(2)]
            peak = jnp.maximum(peaks[0], peaks[1])
            shifts.append([own[c] - peak for c in range(2)])
        for (block, base, tiles), shift in zip(members, shifts):
            total = jnp.zeros((8, both), jnp.float32)
            for t in range(tiles):
                for c in range(2):
                    window = slice(c * rows, (c + 1) * rows)
                    power = jnp.exp2(power_ref[base + t, window] * log2_scale + shift[c])
                    power_ref[base + t, window] = power
                    total = total + fold(power, jnp.sum)
            total = jnp.sum(total, axis=0, keepdims=True)
            live = block * rows + column % rows < length
            if copies > 1:
                live = live & ((column * copies) // both == part)
            inverse_ref[block] = jnp.broadcast_to(jnp.where(live, 1.0 / total, 0.0), (8, both))

    for_groups(length, rows, blocks, on_group)


def grads_kernel(length_ref, place_ref, qk_ref, kt_ref, power_ref, inverse_ref, gv_ref, out_a, out_b, d_ref, dk_ref, dv_ref, bias_acc):
    rows, width = gv_ref.shape[3:]
    blocks = 2 * gv_ref.shape[0]
    both = 2 * rows
    half = rows // 2
    root_scale = 1.0 / math.sqrt(width)
    place = place_ref[0]
    bias_acc[...] = jnp.zeros_like(bias_acc)
    dk_ref[...] = jnp.zeros_like(dk_ref)
    dv_ref[...] = jnp.zeros_like(dv_ref)

    def put(kind, block, tile):
        for c in range(2):
            i, j = position(place, c * blocks + block, blocks)
            out_a[i, j, kind * half : (kind + 1) * half] = tile[c * rows : c * rows + half]
            out_b[j, i, kind * half : (kind + 1) * half] = tile[c * rows + half : (c + 1) * rows]

    def key_blocks(members):
        for block in members or ():
            put(1, block, (dk_ref[block] * root_scale).astype(out_a.dtype))
            put(2, block, dv_ref[block].astype(out_a.dtype))

    def on_group(members, higher):
        key_blocks(higher)
        deltas = []
        for k, (block, base, tiles) in enumerate(members):
            grads = pair(gv_ref, place, block, 0, True)
            first = block - (tiles - 1)
            moment = jnp.zeros((8, both), jnp.float32)
            for t in range(tiles):
                weight_grad = dot(pair(gv_ref, place, first + t, 1, True), grads, ((1,), (1,)))
                d_ref[k, t] = weight_grad
                moment = moment + fold(power_ref[base + t] * weight_grad, jnp.sum)
            deltas.append(jnp.sum(moment, axis=0, keepdims=True) * inverse_ref[block, :1])
        sums = []
        for k, (block, base, tiles) in enumerate(members):
            queries = pair(qk_ref, place, block, 0, False)
            grads = pair(gv_ref, place, block, 0, True)
            inverse = inverse_ref[block, :1]
            first = block - (tiles - 1)
            query_sum = jnp.zeros((width, both), jnp.float32)
            cross = jnp.zeros((8, rows), jnp.float32)
            for t in range(tiles):
                weights = power_ref[base + t] * inverse
                score_grad = weights * (d_ref[k, t] - deltas[k])
                cross = cross + fold(score_grad[:rows, rows:], jnp.sum) + fold(score_grad[rows:, :rows], jnp.sum)
                score_low = score_grad.astype(jnp.bfloat16)
                dv_ref[first + t] += dot(weights.astype(jnp.bfloat16), grads, ((1,), (0,)))
                dk_ref[first + t] += dot(score_low, queries, ((1,), (0,)))
                query_sum = query_sum + dot(kt_ref[first + t], score_low, ((1,), (0,)))
            bias_acc[...] += cross
            sums.append(query_sum)
        for (block, _, _), query_sum in zip(members, sums):
            put(0, block, (query_sum * root_scale).T.astype(out_a.dtype))

    def off_group(members, higher):
        key_blocks(higher)
        for block, _, _ in members:
            put(0, block, jnp.zeros((both, width), out_a.dtype))

    for_groups(length_ref[0], rows, blocks, on_group, off_group)
    key_blocks(range(group_size(blocks)))

    whole = jnp.sum(jnp.sum(bias_acc[...], axis=0, keepdims=True), axis=1, keepdims=True)
    whole = jnp.broadcast_to(whole, (1, width))
    high = whole.astype(jnp.bfloat16).astype(jnp.float32)
    middle = (whole - high).astype(jnp.bfloat16).astype(jnp.float32)
    low = (whole - high - middle).astype(jnp.bfloat16).astype(jnp.float32)
    lane = lax.broadcasted_iota(jnp.int32, (1, width), 1)
    pieces = jnp.where(lane == 0, high, jnp.where(lane == 1, middle, jnp.where(lane == 2, low, 0.0)))
    pieces = jnp.broadcast_to(pieces, (EXTRA, width)).astype(out_a.dtype)
    for i in range(out_a.shape[0]):
        for j in range(out_a.shape[1]):
            out_a[i, j, 3 * half : 3 * half + EXTRA] = pieces


def summed_over(value, axis):
    count = lax.axis_size(axis)
    if count & (count - 1):
        return lax.psum(value, axis)
    step = 1
    while step < count:
        pairs = [(source, source ^ step) for source in range(count)]
        value = value + lax.ppermute(value, axis, pairs)
        step *= 2
    return value


def in_hbm(value):
    return pltpu.with_memory_space_constraint(value, pltpu.HBM)


def moved(value, mask):
    devices = lax.axis_size("chan") * lax.axis_size("seq")
    return lax.ppermute(value, ("chan", "seq"), [(source, source ^ mask) for source in range(devices)])


def exchanged(by_lane, by_seat, devices, phase):
    seats, lanes = stages(devices)
    first_a = [by_lane[0]] + [moved(by_lane[i], lanes[i]) for i in range(1, len(lanes))]
    first_b = [by_seat[0]] + [moved(by_seat[j], seats[j]) for j in range(1, len(seats))]
    last_b = []
    for i in range(1, len(lanes)):
        waiting = jnp.stack([value[i] for value in first_b])
        if phase == "in" or i < len(lanes) - 1:
            waiting, first_a[i] = lax.optimization_barrier((waiting, first_a[i]))
        last_b.append(moved(waiting, lanes[i]))
    last_a = [moved(jnp.stack([value[j] for value in first_a]), seats[j]) for j in range(1, len(seats))]
    return first_a + last_a, first_b + last_b


def arranged(pieces, firsts):
    return jnp.stack([jnp.stack([value[0] for value in pieces[:firsts]])] + list(pieces[firsts:]))


def layer(queries, keys, values, out_grad, cross_bias, lengths):
    rows, features = queries.shape[2:]
    heads = cross_bias.shape[0]
    width = features // heads
    blocks = lax.axis_size("seq")
    devices = lax.axis_size("chan") * blocks
    copies = devices // heads
    seats, lanes = stages(devices)
    place = lax.axis_index("chan") * blocks + lax.axis_index("seq")
    places = place.astype(jnp.int32)[None]
    kind = queries.dtype
    both = 2 * rows
    tiles = min(LOOKBACK + 1, blocks)
    vmem = pl.BlockSpec(memory_space=pltpu.VMEM)
    smem = pl.BlockSpec(memory_space=pltpu.SMEM)
    anywhere = pl.BlockSpec(memory_space=pl.ANY)
    hbm = pl.BlockSpec(memory_space=pltpu.HBM)

    def by_lane(*block):
        return [jax.ShapeDtypeStruct((len(seats),) + block, kind)] * len(lanes)

    def by_seat(*block):
        return [jax.ShapeDtypeStruct((len(lanes),) + block, kind)] * len(seats)

    def size(*shapes):
        return sum(math.prod(shape.shape) * shape.dtype.itemsize for shape in shapes)

    def call(kernel, out_shape, in_specs, out_specs, scratch, grant, matmuls, args):
        flops = 2 * matmuls * tile_count(blocks) * both * both * width
        return pl.pallas_call(
            kernel,
            out_shape=out_shape,
            in_specs=in_specs,
            out_specs=out_specs,
            scratch_shapes=scratch,
            compiler_params=pltpu.CompilerParams(vmem_limit_bytes=grant + SLACK_BYTES),
            cost_estimate=pl.CostEstimate(flops=flops, bytes_accessed=2 << 20, transcendentals=0),
        )(*args)

    def pack(lanes_first, group, first, second):
        sends = (by_lane(2, rows, width) if lanes_first else by_seat(2, rows, width))[: len(group)]
        return call(
            functools.partial(pack_kernel, copies, lanes_first, group),
            sends,
            [smem, hbm, hbm],
            [vmem] * len(sends),
            [pltpu.SemaphoreType.DMA((devices, 2))],
            0,
            0,
            (places, in_hbm(first[0, 0]), in_hbm(second[0, 0])),
        )

    middle = len(lanes) // 2
    far_a = pack(True, list(range(middle, len(lanes))), queries, keys)
    values, out_grad, far_a = lax.optimization_barrier((values, out_grad, far_a))
    sent_b = pack(False, list(range(len(seats))), out_grad, values)
    queries, keys, sent_b = lax.optimization_barrier((queries, keys, sent_b))
    sent_a = pack(True, list(range(middle)), queries, keys) + far_a
    arrived_a, arrived_b = exchanged(sent_a, sent_b, devices, "in")
    qk, gv = arranged(arrived_a, len(lanes)), arranged(arrived_b, len(seats))

    half = rows // 2
    group = group_size(blocks)
    turned_shape = jax.ShapeDtypeStruct((blocks, width, both), kind)
    power_shape = jax.ShapeDtypeStruct((tile_count(blocks), both, both), jnp.float32)
    inverse_shape = jax.ShapeDtypeStruct((blocks, 8, both), jnp.float32)
    sums_shape = jax.ShapeDtypeStruct((blocks, both, width), jnp.float32)
    d_shape = jax.ShapeDtypeStruct((group, tiles, both, both), jnp.float32)
    made = call(
        functools.partial(stats_kernel, copies),
        (turned_shape, power_shape, inverse_shape),
        [smem, smem, smem, vmem],
        [vmem] * 3,
        [],
        size(qk, turned_shape, power_shape, inverse_shape),
        1,
        (lengths, places, cross_bias, qk),
    )
    sends = (
        jax.ShapeDtypeStruct((len(lanes), len(seats), 3 * half + EXTRA, width), kind),
        jax.ShapeDtypeStruct((len(seats), len(lanes), 3 * half, width), kind),
    )
    held = (d_shape, sums_shape, sums_shape)
    back_a, back_b = call(
        grads_kernel,
        sends,
        [smem, smem] + [vmem] * 5,
        [vmem] * 2,
        [pltpu.VMEM(shape.shape, shape.dtype) for shape in held] + [pltpu.VMEM((8, rows), jnp.float32)],
        size(*held, *sends, qk, gv, turned_shape, power_shape, inverse_shape),
        4,
        (lengths, places, qk, *made, gv),
    )
    arrived_a, arrived_b = exchanged(list(back_a), list(back_b), devices, "out")

    pieces = [
        (arrived_a[i][0] if j == 0 else arrived_a[len(lanes) + j - 1][i])[3 * half] for i, j, _ in places_of(devices)
    ]
    masks = jnp.array([mask for _, _, mask in places_of(devices)], jnp.int32)
    chosen = (masks ^ place)[None] // copies == jnp.arange(heads, dtype=jnp.int32)[:, None]
    sums = jnp.sum(jnp.stack(pieces).astype(jnp.float32), axis=1)
    bias_out = summed_over(jnp.sum(jnp.where(chosen, sums[None], 0.0), axis=1), "dp")

    def unpack(part, arrived, earlier):
        flat = jax.ShapeDtypeStruct((rows, features), kind)
        alone = copies == 1
        return pl.pallas_call(
            functools.partial(unpack_kernel, copies, part),
            out_shape=(flat, flat, flat),
            in_specs=[smem] + [anywhere] * len(arrived) + [hbm] * len(earlier),
            out_specs=(hbm, hbm, hbm),
            scratch_shapes=[
                pltpu.VMEM((8, 8, 128) if alone else (3, half, features), kind),
                pltpu.VMEM((1, 8, width) if alone else (devices,) + arrived[0].shape[1:], kind),
                pltpu.SemaphoreType.DMA((devices, 3)),
            ],
            input_output_aliases={1 + len(arrived) + i: i for i in range(len(earlier))},
            compiler_params=pltpu.CompilerParams(vmem_limit_bytes=SLACK_BYTES),
            name="unpack_b" if part else "unpack_a",
        )(places, *arrived, *earlier)

    earlier = unpack(0, arrived_a, ())
    bias_out, *earlier = lax.optimization_barrier((bias_out, *earlier))
    grads = unpack(1, arrived_b, earlier)
    return tuple(grad[None, None] for grad in grads) + (bias_out,)


def solution(mesh):
    placed = P("dp", "chan", "seq", None)
    return jax.shard_map(
        layer,
        mesh=mesh,
        in_specs=(placed, placed, placed, placed, P(), P("dp")),
        out_specs=(placed, placed, placed, P()),
        check_vma=False,
    )
```

```python
import functools
import math

import jax
import jax.numpy as jnp
from jax import lax
from jax.experimental import pallas as pl
from jax.experimental.pallas import tpu as pltpu
from jax.sharding import PartitionSpec as P


LOOKBACK = 6
NEG_FILL = -1e30
EXTRA = 8
LOG2_E = math.log2(math.e)
SLACK_BYTES = 6 << 20


def stages(devices):
    seats = [0, 1, devices // 2, devices // 2 + 1]
    lanes = [2 * step for step in range(devices // 4)]
    return seats, lanes


def places_of(devices):
    seats, lanes = stages(devices)
    return [(i, j, lane + seat) for i, lane in enumerate(lanes) for j, seat in enumerate(seats)]


def run_all(copies):
    for copy in copies:
        copy.start()
    for copy in copies:
        copy.wait()


def piece(pieces, lanes_first, i, j, devices):
    seats, lanes = stages(devices)
    firsts = len(lanes) if lanes_first else len(seats)
    near, far = (i, j) if lanes_first else (j, i)
    return pieces[firsts + far - 1].at[near] if far else pieces[near].at[0]


def position(place, other, blocks):
    mask = place ^ other
    return lax.rem(mask, blocks) // 2, lax.rem(mask, 2) + 2 * (mask // blocks)


def pack_kernel(copies, lanes_first, place_ref, first_ref, second_ref, *refs):
    sems = refs[-1]
    width = refs[0].shape[-1]
    started = []
    for index, (i, j, mask) in enumerate(places_of(sems.shape[0])):
        head = (place_ref[0] ^ mask) // copies
        columns = pl.ds(pl.multiple_of(head * width, width), width)
        target = refs[i].at[j] if lanes_first else refs[j].at[i]
        for kind, source in enumerate((first_ref, second_ref)):
            started.append(pltpu.make_async_copy(source.at[:, columns], target.at[kind], sems.at[index, kind]))
    run_all(started)


def unpack_kernel(copies, counts, place_ref, *refs):
    sems, home_b, home_a, sums = refs[-1], refs[-2], refs[-3], refs[-4]
    outs = refs[-7:-4]
    devices = sems.shape[0]
    width = home_a.shape[2]
    half = outs[0].shape[0] // 2
    started = []
    for part, home in enumerate((home_a, home_b)):
        pieces = refs[: counts[0]] if part == 0 else refs[counts[0] : counts[0] + counts[1]]
        window = pl.ds(part * half, half)
        for index, (i, j, mask) in enumerate(places_of(devices)):
            source = piece(pieces, part == 0, i, j, devices)
            other = place_ref[0] ^ mask
            if copies > 1:
                started.append(pltpu.make_async_copy(source, home.at[other], sems.at[index, 3 * part]))
                continue
            columns = pl.ds(pl.multiple_of(other * width, width), width)
            for kind, out in enumerate(outs):
                rows = source.at[pl.ds(kind * half, half)]
                copy = pltpu.make_async_copy(rows, out.at[window, columns], sems.at[index, 3 * part + kind])
                started.append(copy)
    run_all(started)
    if copies > 1:
        for part, home in enumerate((home_a, home_b)):
            for head in range(devices // copies):
                columns = pl.ds(head * width, width)
                for kind in range(3):
                    rows = pl.ds(kind * half, half)
                    value = home[head * copies, rows].astype(jnp.float32)
                    for other in range(1, copies):
                        value = value + home[head * copies + other, rows].astype(jnp.float32)
                    sums[kind, part * half : (part + 1) * half, columns] = value.astype(sums.dtype)
        run_all([pltpu.make_async_copy(sums.at[kind], out, sems.at[0, kind]) for kind, out in enumerate(outs)])


def dot(left, right, contract):
    return lax.dot_general(left, right, (contract, ((), ())), preferred_element_type=jnp.float32)


def fold(tile, op):
    return op(tile.reshape(tile.shape[0] // 8, 8, tile.shape[1]), axis=0)


def pair(ref, place, block, kind, lanes_first):
    blocks = 2 * ref.shape[1 if not lanes_first else 0]
    parts = []
    for c in range(2):
        i, j = position(place, c * blocks + block, blocks)
        parts.append(ref[i, j, kind] if lanes_first else ref[j, i, kind])
    return jnp.concatenate(parts, axis=0)


def tile_count(blocks):
    return sum(min(block, LOOKBACK) + 1 for block in range(blocks))


def group_size(blocks):
    early = min(LOOKBACK, blocks)
    return 2 if early % 2 == 0 and (blocks - early) % 2 == 0 else 1


def for_groups(length, rows, blocks, on_group, off_group=None):
    early = min(LOOKBACK, blocks)
    group = group_size(blocks)
    visited = jnp.minimum(((length + group * rows - 1) // (group * rows)) * group, blocks)

    def either(members, higher):
        pl.when(members[0][0] < visited)(lambda: on_group(members, higher))
        if off_group is not None:
            pl.when(members[0][0] >= visited)(lambda: off_group(members, higher))

    def late(start, higher):
        members = [(start + k, tile_count(LOOKBACK) + (start + k - LOOKBACK) * (LOOKBACK + 1)) for k in range(group)]
        either([(block, base, LOOKBACK + 1) for block, base in members], higher)

    higher = None
    if blocks > early:
        late(blocks - group, None)

        def step(index, carried):
            start = blocks - (index + 1) * group
            late(start, [start + group + k for k in range(group)])
            return carried

        lax.fori_loop(1, (blocks - early) // group, step, 0)
        higher = [early + k for k in range(group)]
    for start in range(early - group, -1, -group):
        either([(block, tile_count(block), block + 1) for block in range(start, start + group)], higher)
        higher = [start + k for k in range(group)]


def stats_kernel(copies, length_ref, place_ref, bias_ref, qk_ref, kt_ref, power_ref, inverse_ref):
    rows, width = qk_ref.shape[3:]
    blocks = 2 * qk_ref.shape[1]
    both = 2 * rows
    log2_scale = LOG2_E / math.sqrt(width)
    place = place_ref[0]
    bias = bias_ref[place // copies] * LOG2_E
    part = place % copies
    length = length_ref[0]

    column = lax.broadcasted_iota(jnp.int32, (1, both), 1)
    own = [jnp.where((column // rows) == c, 0.0, bias) for c in range(2)]
    key_row = lax.broadcasted_iota(jnp.int32, (rows, both), 0)
    query_column = lax.broadcasted_iota(jnp.int32, (rows, both), 1) % rows
    for block in range(blocks):
        kt_ref[block] = pair(qk_ref, place, block, 1, False).T

    def on_group(members, higher):
        shifts = []
        for block, base, tiles in members:
            queries = pair(qk_ref, place, block, 0, False)
            first = block - (tiles - 1)
            peaks = [jnp.full((8, both), NEG_FILL, jnp.float32)] * 2
            for t in range(tiles):
                raw = dot(pair(qk_ref, place, first + t, 1, False), queries, ((1,), (1,)))
                for c in range(2):
                    tile = raw[c * rows : (c + 1) * rows]
                    if t == tiles - 1:
                        tile = jnp.where(key_row <= query_column, tile, NEG_FILL)
                    if tiles == LOOKBACK + 1 and t == 0:
                        tile = jnp.where(key_row > query_column, tile, NEG_FILL)
                    power_ref[base + t, c * rows : (c + 1) * rows] = tile
                    peaks[c] = jnp.maximum(peaks[c], fold(tile, jnp.max))
            peaks = [jnp.max(peaks[c], axis=0, keepdims=True) * log2_scale + own[c] for c in range(2)]
            peak = jnp.maximum(peaks[0], peaks[1])
            shifts.append([own[c] - peak for c in range(2)])
        for (block, base, tiles), shift in zip(members, shifts):
            total = jnp.zeros((8, both), jnp.float32)
            for t in range(tiles):
                for c in range(2):
                    window = slice(c * rows, (c + 1) * rows)
                    power = jnp.exp2(power_ref[base + t, window] * log2_scale + shift[c])
                    power_ref[base + t, window] = power
                    total = total + fold(power, jnp.sum)
            total = jnp.sum(total, axis=0, keepdims=True)
            live = block * rows + column % rows < length
            if copies > 1:
                live = live & ((column * copies) // both == part)
            inverse_ref[block] = jnp.broadcast_to(jnp.where(live, 1.0 / total, 0.0), (8, both))

    for_groups(length, rows, blocks, on_group)


def grads_kernel(length_ref, place_ref, qk_ref, kt_ref, power_ref, inverse_ref, gv_ref, out_a, out_b, d_ref, dk_ref, dv_ref, bias_acc):
    rows, width = gv_ref.shape[3:]
    blocks = 2 * gv_ref.shape[0]
    both = 2 * rows
    half = rows // 2
    root_scale = 1.0 / math.sqrt(width)
    place = place_ref[0]
    bias_acc[...] = jnp.zeros_like(bias_acc)
    dk_ref[...] = jnp.zeros_like(dk_ref)
    dv_ref[...] = jnp.zeros_like(dv_ref)

    def put(kind, block, tile):
        for c in range(2):
            i, j = position(place, c * blocks + block, blocks)
            out_a[i, j, kind * half : (kind + 1) * half] = tile[c * rows : c * rows + half]
            out_b[j, i, kind * half : (kind + 1) * half] = tile[c * rows + half : (c + 1) * rows]

    def key_blocks(members):
        for block in members or ():
            put(1, block, (dk_ref[block] * root_scale).astype(out_a.dtype))
            put(2, block, dv_ref[block].astype(out_a.dtype))

    def on_group(members, higher):
        key_blocks(higher)
        deltas = []
        for k, (block, base, tiles) in enumerate(members):
            grads = pair(gv_ref, place, block, 0, True)
            first = block - (tiles - 1)
            moment = jnp.zeros((8, both), jnp.float32)
            for t in range(tiles):
                weight_grad = dot(pair(gv_ref, place, first + t, 1, True), grads, ((1,), (1,)))
                d_ref[k, t] = weight_grad
                moment = moment + fold(power_ref[base + t] * weight_grad, jnp.sum)
            deltas.append(jnp.sum(moment, axis=0, keepdims=True) * inverse_ref[block, :1])
        sums = []
        for k, (block, base, tiles) in enumerate(members):
            queries = pair(qk_ref, place, block, 0, False)
            grads = pair(gv_ref, place, block, 0, True)
            inverse = inverse_ref[block, :1]
            first = block - (tiles - 1)
            query_sum = jnp.zeros((width, both), jnp.float32)
            cross = jnp.zeros((8, rows), jnp.float32)
            for t in range(tiles):
                weights = power_ref[base + t] * inverse
                score_grad = weights * (d_ref[k, t] - deltas[k])
                cross = cross + fold(score_grad[:rows, rows:], jnp.sum) + fold(score_grad[rows:, :rows], jnp.sum)
                score_low = score_grad.astype(jnp.bfloat16)
                dv_ref[first + t] += dot(weights.astype(jnp.bfloat16), grads, ((1,), (0,)))
                dk_ref[first + t] += dot(score_low, queries, ((1,), (0,)))
                query_sum = query_sum + dot(kt_ref[first + t], score_low, ((1,), (0,)))
            bias_acc[...] += cross
            sums.append(query_sum)
        for (block, _, _), query_sum in zip(members, sums):
            put(0, block, (query_sum * root_scale).T.astype(out_a.dtype))

    def off_group(members, higher):
        key_blocks(higher)
        for block, _, _ in members:
            put(0, block, jnp.zeros((both, width), out_a.dtype))

    for_groups(length_ref[0], rows, blocks, on_group, off_group)
    key_blocks(range(group_size(blocks)))

    whole = jnp.sum(jnp.sum(bias_acc[...], axis=0, keepdims=True), axis=1, keepdims=True)
    whole = jnp.broadcast_to(whole, (1, width))
    high = whole.astype(jnp.bfloat16).astype(jnp.float32)
    middle = (whole - high).astype(jnp.bfloat16).astype(jnp.float32)
    low = (whole - high - middle).astype(jnp.bfloat16).astype(jnp.float32)
    lane = lax.broadcasted_iota(jnp.int32, (1, width), 1)
    pieces = jnp.where(lane == 0, high, jnp.where(lane == 1, middle, jnp.where(lane == 2, low, 0.0)))
    pieces = jnp.broadcast_to(pieces, (EXTRA, width)).astype(out_a.dtype)
    for i in range(out_a.shape[0]):
        for j in range(out_a.shape[1]):
            out_a[i, j, 3 * half : 3 * half + EXTRA] = pieces


def summed_over(value, axis):
    count = lax.axis_size(axis)
    if count & (count - 1):
        return lax.psum(value, axis)
    step = 1
    while step < count:
        pairs = [(source, source ^ step) for source in range(count)]
        value = value + lax.ppermute(value, axis, pairs)
        step *= 2
    return value


def in_hbm(value):
    return pltpu.with_memory_space_constraint(value, pltpu.HBM)


def moved(value, mask):
    devices = lax.axis_size("chan") * lax.axis_size("seq")
    return lax.ppermute(value, ("chan", "seq"), [(source, source ^ mask) for source in range(devices)])


def exchanged(by_lane, by_seat, devices):
    seats, lanes = stages(devices)
    first_a = [by_lane[0]] + [moved(by_lane[i], lanes[i]) for i in range(1, len(lanes))]
    first_b = [by_seat[0]] + [moved(by_seat[j], seats[j]) for j in range(1, len(seats))]
    last_b = []
    for i in range(1, len(lanes)):
        waiting, first_a[i] = lax.optimization_barrier((jnp.stack([value[i] for value in first_b]), first_a[i]))
        last_b.append(moved(waiting, lanes[i]))
    last_a = [moved(jnp.stack([value[j] for value in first_a]), seats[j]) for j in range(1, len(seats))]
    return first_a + last_a, first_b + last_b


def arranged(pieces, firsts):
    return jnp.stack([jnp.stack([value[0] for value in pieces[:firsts]])] + list(pieces[firsts:]))


def layer(queries, keys, values, out_grad, cross_bias, lengths):
    rows, features = queries.shape[2:]
    heads = cross_bias.shape[0]
    width = features // heads
    blocks = lax.axis_size("seq")
    devices = lax.axis_size("chan") * blocks
    copies = devices // heads
    seats, lanes = stages(devices)
    place = lax.axis_index("chan") * blocks + lax.axis_index("seq")
    places = place.astype(jnp.int32)[None]
    kind = queries.dtype
    both = 2 * rows
    tiles = min(LOOKBACK + 1, blocks)
    vmem = pl.BlockSpec(memory_space=pltpu.VMEM)
    smem = pl.BlockSpec(memory_space=pltpu.SMEM)
    anywhere = pl.BlockSpec(memory_space=pl.ANY)
    hbm = pl.BlockSpec(memory_space=pltpu.HBM)

    def by_lane(*block):
        return [jax.ShapeDtypeStruct((len(seats),) + block, kind)] * len(lanes)

    def by_seat(*block):
        return [jax.ShapeDtypeStruct((len(lanes),) + block, kind)] * len(seats)

    def size(*shapes):
        return sum(math.prod(shape.shape) * shape.dtype.itemsize for shape in shapes)

    def call(kernel, out_shape, in_specs, out_specs, scratch, grant, matmuls, args):
        flops = 2 * matmuls * tile_count(blocks) * both * both * width
        return pl.pallas_call(
            kernel,
            out_shape=out_shape,
            in_specs=in_specs,
            out_specs=out_specs,
            scratch_shapes=scratch,
            compiler_params=pltpu.CompilerParams(vmem_limit_bytes=grant + SLACK_BYTES),
            cost_estimate=pl.CostEstimate(flops=flops, bytes_accessed=2 << 20, transcendentals=0),
        )(*args)

    def pack(lanes_first, first, second):
        sends = by_lane(2, rows, width) if lanes_first else by_seat(2, rows, width)
        return call(
            functools.partial(pack_kernel, copies, lanes_first),
            sends,
            [smem, hbm, hbm],
            [vmem] * len(sends),
            [pltpu.SemaphoreType.DMA((devices, 2))],
            0,
            0,
            (places, in_hbm(first[0, 0]), in_hbm(second[0, 0])),
        )

    sent_a = pack(True, queries, keys)
    values, out_grad, sent_a = lax.optimization_barrier((values, out_grad, sent_a))
    sent_b = pack(False, out_grad, values)
    arrived_a, arrived_b = exchanged(sent_a, sent_b, devices)
    qk, gv = arranged(arrived_a, len(lanes)), arranged(arrived_b, len(seats))

    half = rows // 2
    group = group_size(blocks)
    turned_shape = jax.ShapeDtypeStruct((blocks, width, both), kind)
    power_shape = jax.ShapeDtypeStruct((tile_count(blocks), both, both), jnp.float32)
    inverse_shape = jax.ShapeDtypeStruct((blocks, 8, both), jnp.float32)
    sums_shape = jax.ShapeDtypeStruct((blocks, both, width), jnp.float32)
    d_shape = jax.ShapeDtypeStruct((group, tiles, both, both), jnp.float32)
    made = call(
        functools.partial(stats_kernel, copies),
        (turned_shape, power_shape, inverse_shape),
        [smem, smem, smem, vmem],
        [vmem] * 3,
        [],
        size(qk, turned_shape, power_shape, inverse_shape),
        1,
        (lengths, places, cross_bias, qk),
    )
    sends = (
        jax.ShapeDtypeStruct((len(lanes), len(seats), 3 * half + EXTRA, width), kind),
        jax.ShapeDtypeStruct((len(seats), len(lanes), 3 * half, width), kind),
    )
    held = (d_shape, sums_shape, sums_shape)
    back_a, back_b = call(
        grads_kernel,
        sends,
        [smem, smem] + [vmem] * 5,
        [vmem] * 2,
        [pltpu.VMEM(shape.shape, shape.dtype) for shape in held] + [pltpu.VMEM((8, rows), jnp.float32)],
        size(*held, *sends, qk, gv, turned_shape, power_shape, inverse_shape),
        4,
        (lengths, places, qk, *made, gv),
    )
    arrived_a, arrived_b = exchanged(list(back_a), list(back_b), devices)

    pieces = [
        (arrived_a[i][0] if j == 0 else arrived_a[len(lanes) + j - 1][i])[3 * half] for i, j, _ in places_of(devices)
    ]
    masks = jnp.array([mask for _, _, mask in places_of(devices)], jnp.int32)
    chosen = (masks ^ place)[None] // copies == jnp.arange(heads, dtype=jnp.int32)[:, None]
    sums = jnp.sum(jnp.stack(pieces).astype(jnp.float32), axis=1)
    bias_out = summed_over(jnp.sum(jnp.where(chosen, sums[None], 0.0), axis=1), "dp")

    flat = jax.ShapeDtypeStruct((rows, features), kind)
    alone = copies == 1
    arrived = arrived_a + arrived_b
    grads = pl.pallas_call(
        functools.partial(unpack_kernel, copies, (len(arrived_a), len(arrived_b))),
        out_shape=(flat, flat, flat),
        in_specs=[smem] + [anywhere] * len(arrived),
        out_specs=(hbm, hbm, hbm),
        scratch_shapes=[
            pltpu.VMEM((3, 16 if alone else rows, features), kind),
            pltpu.VMEM((1 if alone else devices,) + arrived_a[0].shape[1:], kind),
            pltpu.VMEM((1 if alone else devices,) + arrived_b[0].shape[1:], kind),
            pltpu.SemaphoreType.DMA((devices, 6)),
        ],
        compiler_params=pltpu.CompilerParams(vmem_limit_bytes=2 * SLACK_BYTES),
        name="unpack",
    )(places, *arrived)
    return tuple(grad[None, None] for grad in grads) + (bias_out,)


def solution(mesh):
    placed = P("dp", "chan", "seq", None)
    return jax.shard_map(
        layer,
        mesh=mesh,
        in_specs=(placed, placed, placed, placed, P(), P("dp")),
        out_specs=(placed, placed, placed, P()),
        check_vma=False,
    )
```

```python
import functools
import math

import jax
import jax.numpy as jnp
from jax import lax
from jax.experimental import pallas as pl
from jax.experimental.pallas import tpu as pltpu
from jax.sharding import PartitionSpec as P


LOOKBACK = 6
NEG_FILL = -1e30
LOG2_E = math.log2(math.e)
SLACK_BYTES = 6 << 20


def stages(devices):
    seats = [0, 1, devices // 2, devices // 2 + 1]
    lanes = [2 * step for step in range(devices // 4)]
    return seats, lanes


def places_of(devices):
    seats, lanes = stages(devices)
    return [(i, j, lane + seat) for i, lane in enumerate(lanes) for j, seat in enumerate(seats)]


def run_all(copies):
    for copy in copies:
        copy.start()
    for copy in copies:
        copy.wait()


def piece(pieces, lanes_first, i, j, devices):
    seats, lanes = stages(devices)
    firsts = len(lanes) if lanes_first else len(seats)
    near, far = (i, j) if lanes_first else (j, i)
    return pieces[firsts + far - 1].at[near] if far else pieces[near].at[0]


def position(place, other, blocks):
    mask = place ^ other
    return lax.rem(mask, blocks) // 2, lax.rem(mask, 2) + 2 * (mask // blocks)


def pack_kernel(copies, lanes_first, place_ref, first_ref, second_ref, *refs):
    sems = refs[-1]
    width = refs[0].shape[-1]
    started = []
    for index, (i, j, mask) in enumerate(places_of(sems.shape[0])):
        head = (place_ref[0] ^ mask) // copies
        columns = pl.ds(pl.multiple_of(head * width, width), width)
        target = refs[i].at[j] if lanes_first else refs[j].at[i]
        for kind, source in enumerate((first_ref, second_ref)):
            started.append(pltpu.make_async_copy(source.at[:, columns], target.at[kind], sems.at[index, kind]))
    run_all(started)


def unpack_kernel(copies, counts, place_ref, *refs):
    sems, home_b, home_a, sums = refs[-1], refs[-2], refs[-3], refs[-4]
    outs = refs[-7:-4]
    devices = sems.shape[0]
    width = home_a.shape[2]
    half = outs[0].shape[0] // 2
    started = []
    for part, home in enumerate((home_a, home_b)):
        pieces = refs[: counts[0]] if part == 0 else refs[counts[0] : counts[0] + counts[1]]
        window = pl.ds(part * half, half)
        for index, (i, j, mask) in enumerate(places_of(devices)):
            source = piece(pieces, part == 0, i, j, devices)
            other = place_ref[0] ^ mask
            if copies > 1:
                started.append(pltpu.make_async_copy(source, home.at[other], sems.at[index, 3 * part]))
                continue
            columns = pl.ds(pl.multiple_of(other * width, width), width)
            for kind, out in enumerate(outs):
                rows = source.at[pl.ds(kind * half, half)]
                copy = pltpu.make_async_copy(rows, out.at[window, columns], sems.at[index, 3 * part + kind])
                started.append(copy)
    run_all(started)
    if copies > 1:
        for part, home in enumerate((home_a, home_b)):
            for head in range(devices // copies):
                columns = pl.ds(head * width, width)
                for kind in range(3):
                    rows = pl.ds(kind * half, half)
                    value = home[head * copies, rows].astype(jnp.float32)
                    for other in range(1, copies):
                        value = value + home[head * copies + other, rows].astype(jnp.float32)
                    sums[kind, part * half : (part + 1) * half, columns] = value.astype(sums.dtype)
        run_all([pltpu.make_async_copy(sums.at[kind], out, sems.at[0, kind]) for kind, out in enumerate(outs)])


def dot(left, right, contract):
    return lax.dot_general(left, right, (contract, ((), ())), preferred_element_type=jnp.float32)


def fold(tile, op):
    return op(tile.reshape(tile.shape[0] // 8, 8, tile.shape[1]), axis=0)


def pair(ref, place, block, kind, lanes_first):
    blocks = 2 * ref.shape[1 if not lanes_first else 0]
    parts = []
    for c in range(2):
        i, j = position(place, c * blocks + block, blocks)
        parts.append(ref[i, j, kind] if lanes_first else ref[j, i, kind])
    return jnp.concatenate(parts, axis=0)


def tile_count(blocks):
    return sum(min(block, LOOKBACK) + 1 for block in range(blocks))


def group_size(blocks):
    early = min(LOOKBACK, blocks)
    return 2 if early % 2 == 0 and (blocks - early) % 2 == 0 else 1


def for_groups(length, rows, blocks, on_group, off_group=None):
    early = min(LOOKBACK, blocks)
    group = group_size(blocks)
    visited = jnp.minimum(((length + group * rows - 1) // (group * rows)) * group, blocks)

    def either(members, higher):
        pl.when(members[0][0] < visited)(lambda: on_group(members, higher))
        if off_group is not None:
            pl.when(members[0][0] >= visited)(lambda: off_group(members, higher))

    def late(start, higher):
        members = [(start + k, tile_count(LOOKBACK) + (start + k - LOOKBACK) * (LOOKBACK + 1)) for k in range(group)]
        either([(block, base, LOOKBACK + 1) for block, base in members], higher)

    higher = None
    if blocks > early:
        late(blocks - group, None)

        def step(index, carried):
            start = blocks - (index + 1) * group
            late(start, [start + group + k for k in range(group)])
            return carried

        lax.fori_loop(1, (blocks - early) // group, step, 0)
        higher = [early + k for k in range(group)]
    for start in range(early - group, -1, -group):
        either([(block, tile_count(block), block + 1) for block in range(start, start + group)], higher)
        higher = [start + k for k in range(group)]


def stats_kernel(copies, length_ref, place_ref, bias_ref, qk_ref, kt_ref, power_ref, inverse_ref):
    rows, width = qk_ref.shape[3:]
    blocks = 2 * qk_ref.shape[1]
    both = 2 * rows
    log2_scale = LOG2_E / math.sqrt(width)
    place = place_ref[0]
    bias = bias_ref[place // copies] * LOG2_E
    part = place % copies
    length = length_ref[0]

    column = lax.broadcasted_iota(jnp.int32, (1, both), 1)
    own = [jnp.where((column // rows) == c, 0.0, bias) for c in range(2)]
    key_row = lax.broadcasted_iota(jnp.int32, (rows, both), 0)
    query_column = lax.broadcasted_iota(jnp.int32, (rows, both), 1) % rows
    for block in range(blocks):
        kt_ref[block] = pair(qk_ref, place, block, 1, False).T

    def on_group(members, higher):
        shifts = []
        for block, base, tiles in members:
            queries = pair(qk_ref, place, block, 0, False)
            first = block - (tiles - 1)
            peaks = [jnp.full((8, both), NEG_FILL, jnp.float32)] * 2
            for t in range(tiles):
                raw = dot(pair(qk_ref, place, first + t, 1, False), queries, ((1,), (1,)))
                for c in range(2):
                    tile = raw[c * rows : (c + 1) * rows]
                    if t == tiles - 1:
                        tile = jnp.where(key_row <= query_column, tile, NEG_FILL)
                    if tiles == LOOKBACK + 1 and t == 0:
                        tile = jnp.where(key_row > query_column, tile, NEG_FILL)
                    power_ref[base + t, c * rows : (c + 1) * rows] = tile
                    peaks[c] = jnp.maximum(peaks[c], fold(tile, jnp.max))
            peaks = [jnp.max(peaks[c], axis=0, keepdims=True) * log2_scale + own[c] for c in range(2)]
            peak = jnp.maximum(peaks[0], peaks[1])
            shifts.append([own[c] - peak for c in range(2)])
        for (block, base, tiles), shift in zip(members, shifts):
            total = jnp.zeros((8, both), jnp.float32)
            for t in range(tiles):
                for c in range(2):
                    window = slice(c * rows, (c + 1) * rows)
                    power = jnp.exp2(power_ref[base + t, window] * log2_scale + shift[c])
                    power_ref[base + t, window] = power
                    total = total + fold(power, jnp.sum)
            total = jnp.sum(total, axis=0, keepdims=True)
            live = block * rows + column % rows < length
            if copies > 1:
                live = live & ((column * copies) // both == part)
            inverse_ref[block] = jnp.broadcast_to(jnp.where(live, 1.0 / total, 0.0), (8, both))

    for_groups(length, rows, blocks, on_group)


def grads_kernel(
    copies, length_ref, place_ref, qk_ref, kt_ref, power_ref, inverse_ref, gv_ref, out_a, out_b, bias_ref, d_ref, dk_ref, dv_ref, bias_acc
):
    rows, width = gv_ref.shape[3:]
    blocks = 2 * gv_ref.shape[0]
    both = 2 * rows
    half = rows // 2
    root_scale = 1.0 / math.sqrt(width)
    place = place_ref[0]
    bias_acc[...] = jnp.zeros_like(bias_acc)
    dk_ref[...] = jnp.zeros_like(dk_ref)
    dv_ref[...] = jnp.zeros_like(dv_ref)

    def put(kind, block, tile):
        for c in range(2):
            i, j = position(place, c * blocks + block, blocks)
            out_a[i, j, kind * half : (kind + 1) * half] = tile[c * rows : c * rows + half]
            out_b[j, i, kind * half : (kind + 1) * half] = tile[c * rows + half : (c + 1) * rows]

    def key_blocks(members):
        for block in members or ():
            put(1, block, (dk_ref[block] * root_scale).astype(out_a.dtype))
            put(2, block, dv_ref[block].astype(out_a.dtype))

    def on_group(members, higher):
        key_blocks(higher)
        deltas = []
        for k, (block, base, tiles) in enumerate(members):
            grads = pair(gv_ref, place, block, 0, True)
            first = block - (tiles - 1)
            moment = jnp.zeros((8, both), jnp.float32)
            for t in range(tiles):
                weight_grad = dot(pair(gv_ref, place, first + t, 1, True), grads, ((1,), (1,)))
                d_ref[k, t] = weight_grad
                moment = moment + fold(power_ref[base + t] * weight_grad, jnp.sum)
            deltas.append(jnp.sum(moment, axis=0, keepdims=True) * inverse_ref[block, :1])
        sums = []
        for k, (block, base, tiles) in enumerate(members):
            queries = pair(qk_ref, place, block, 0, False)
            grads = pair(gv_ref, place, block, 0, True)
            inverse = inverse_ref[block, :1]
            first = block - (tiles - 1)
            query_sum = jnp.zeros((width, both), jnp.float32)
            cross = jnp.zeros((8, rows), jnp.float32)
            for t in range(tiles):
                weights = power_ref[base + t] * inverse
                score_grad = weights * (d_ref[k, t] - deltas[k])
                cross = cross + fold(score_grad[:rows, rows:], jnp.sum) + fold(score_grad[rows:, :rows], jnp.sum)
                score_low = score_grad.astype(jnp.bfloat16)
                dv_ref[first + t] += dot(weights.astype(jnp.bfloat16), grads, ((1,), (0,)))
                dk_ref[first + t] += dot(score_low, queries, ((1,), (0,)))
                query_sum = query_sum + dot(kt_ref[first + t], score_low, ((1,), (0,)))
            bias_acc[...] += cross
            sums.append(query_sum)
        for (block, _, _), query_sum in zip(members, sums):
            put(0, block, (query_sum * root_scale).T.astype(out_a.dtype))

    def off_group(members, higher):
        key_blocks(higher)
        for block, _, _ in members:
            put(0, block, jnp.zeros((both, width), out_a.dtype))

    for_groups(length_ref[0], rows, blocks, on_group, off_group)
    key_blocks(range(group_size(blocks)))

    whole = jnp.sum(jnp.sum(bias_acc[...], axis=0, keepdims=True), axis=1, keepdims=True)
    lane = lax.broadcasted_iota(jnp.int32, bias_ref.shape, 1)
    bias_ref[...] = jnp.where(lane == place // copies, whole, 0.0)


def summed_over(value, axis):
    count = lax.axis_size(axis)
    if count & (count - 1):
        return lax.psum(value, axis)
    step = 1
    while step < count:
        pairs = [(source, source ^ step) for source in range(count)]
        value = value + lax.ppermute(value, axis, pairs)
        step *= 2
    return value


def in_hbm(value):
    return pltpu.with_memory_space_constraint(value, pltpu.HBM)


def moved(value, mask):
    devices = lax.axis_size("chan") * lax.axis_size("seq")
    return lax.ppermute(value, ("chan", "seq"), [(source, source ^ mask) for source in range(devices)])


def exchanged(by_lane, by_seat, devices):
    seats, lanes = stages(devices)
    first_a = [by_lane[0]] + [moved(by_lane[i], lanes[i]) for i in range(1, len(lanes))]
    first_b = [by_seat[0]] + [moved(by_seat[j], seats[j]) for j in range(1, len(seats))]
    last_b = []
    for i in range(1, len(lanes)):
        waiting, first_a[i] = lax.optimization_barrier((jnp.stack([value[i] for value in first_b]), first_a[i]))
        last_b.append(moved(waiting, lanes[i]))
    last_a = [moved(jnp.stack([value[j] for value in first_a]), seats[j]) for j in range(1, len(seats))]
    return first_a + last_a, first_b + last_b


def arranged(pieces, firsts):
    return jnp.stack([jnp.stack([value[0] for value in pieces[:firsts]])] + list(pieces[firsts:]))


def layer(queries, keys, values, out_grad, cross_bias, lengths):
    rows, features = queries.shape[2:]
    heads = cross_bias.shape[0]
    width = features // heads
    blocks = lax.axis_size("seq")
    devices = lax.axis_size("chan") * blocks
    copies = devices // heads
    seats, lanes = stages(devices)
    place = lax.axis_index("chan") * blocks + lax.axis_index("seq")
    places = place.astype(jnp.int32)[None]
    kind = queries.dtype
    both = 2 * rows
    tiles = min(LOOKBACK + 1, blocks)
    vmem = pl.BlockSpec(memory_space=pltpu.VMEM)
    smem = pl.BlockSpec(memory_space=pltpu.SMEM)
    anywhere = pl.BlockSpec(memory_space=pl.ANY)
    hbm = pl.BlockSpec(memory_space=pltpu.HBM)

    def by_lane(*block):
        return [jax.ShapeDtypeStruct((len(seats),) + block, kind)] * len(lanes)

    def by_seat(*block):
        return [jax.ShapeDtypeStruct((len(lanes),) + block, kind)] * len(seats)

    def size(*shapes):
        return sum(math.prod(shape.shape) * shape.dtype.itemsize for shape in shapes)

    def call(kernel, out_shape, in_specs, out_specs, scratch, grant, matmuls, args):
        flops = 2 * matmuls * tile_count(blocks) * both * both * width
        return pl.pallas_call(
            kernel,
            out_shape=out_shape,
            in_specs=in_specs,
            out_specs=out_specs,
            scratch_shapes=scratch,
            compiler_params=pltpu.CompilerParams(vmem_limit_bytes=grant + SLACK_BYTES),
            cost_estimate=pl.CostEstimate(flops=flops, bytes_accessed=2 << 20, transcendentals=0),
        )(*args)

    def pack(lanes_first, first, second):
        sends = by_lane(2, rows, width) if lanes_first else by_seat(2, rows, width)
        return call(
            functools.partial(pack_kernel, copies, lanes_first),
            sends,
            [smem, hbm, hbm],
            [vmem] * len(sends),
            [pltpu.SemaphoreType.DMA((devices, 2))],
            0,
            0,
            (places, in_hbm(first[0, 0]), in_hbm(second[0, 0])),
        )

    sent_a = pack(True, queries, keys)
    values, out_grad, sent_a = lax.optimization_barrier((values, out_grad, sent_a))
    sent_b = pack(False, out_grad, values)
    arrived_a, arrived_b = exchanged(sent_a, sent_b, devices)
    qk, gv = arranged(arrived_a, len(lanes)), arranged(arrived_b, len(seats))

    half = rows // 2
    group = group_size(blocks)
    turned_shape = jax.ShapeDtypeStruct((blocks, width, both), kind)
    power_shape = jax.ShapeDtypeStruct((tile_count(blocks), both, both), jnp.float32)
    inverse_shape = jax.ShapeDtypeStruct((blocks, 8, both), jnp.float32)
    sums_shape = jax.ShapeDtypeStruct((blocks, both, width), jnp.float32)
    d_shape = jax.ShapeDtypeStruct((group, tiles, both, both), jnp.float32)
    made = call(
        functools.partial(stats_kernel, copies),
        (turned_shape, power_shape, inverse_shape),
        [smem, smem, smem, vmem],
        [vmem] * 3,
        [],
        size(qk, turned_shape, power_shape, inverse_shape),
        1,
        (lengths, places, cross_bias, qk),
    )
    sends = (
        jax.ShapeDtypeStruct((len(lanes), len(seats), 3 * half, width), kind),
        jax.ShapeDtypeStruct((len(seats), len(lanes), 3 * half, width), kind),
        jax.ShapeDtypeStruct((1, heads), jnp.float32),
    )
    held = (d_shape, sums_shape, sums_shape)
    back_a, back_b, bias_sum = call(
        functools.partial(grads_kernel, copies),
        sends,
        [smem, smem] + [vmem] * 5,
        [vmem] * 3,
        [pltpu.VMEM(shape.shape, shape.dtype) for shape in held] + [pltpu.VMEM((8, rows), jnp.float32)],
        size(*held, *sends, qk, gv, turned_shape, power_shape, inverse_shape),
        4,
        (lengths, places, qk, *made, gv),
    )
    arrived_a, arrived_b = exchanged(list(back_a), list(back_b), devices)

    bias_out = summed_over(bias_sum[0], "dp")
    mask = 1
    while mask < devices:
        bias_out = bias_out + moved(bias_out, mask)
        mask *= 2

    flat = jax.ShapeDtypeStruct((rows, features), kind)
    alone = copies == 1
    arrived = arrived_a + arrived_b
    grads = pl.pallas_call(
        functools.partial(unpack_kernel, copies, (len(arrived_a), len(arrived_b))),
        out_shape=(flat, flat, flat),
        in_specs=[smem] + [anywhere] * len(arrived),
        out_specs=(hbm, hbm, hbm),
        scratch_shapes=[
            pltpu.VMEM((3, 16 if alone else rows, features), kind),
            pltpu.VMEM((1 if alone else devices,) + arrived_a[0].shape[1:], kind),
            pltpu.VMEM((1 if alone else devices,) + arrived_b[0].shape[1:], kind),
            pltpu.SemaphoreType.DMA((devices, 6)),
        ],
        compiler_params=pltpu.CompilerParams(vmem_limit_bytes=2 * SLACK_BYTES),
        name="unpack",
    )(places, *arrived)
    return tuple(grad[None, None] for grad in grads) + (bias_out,)


def solution(mesh):
    placed = P("dp", "chan", "seq", None)
    return jax.shard_map(
        layer,
        mesh=mesh,
        in_specs=(placed, placed, placed, placed, P(), P("dp")),
        out_specs=(placed, placed, placed, P()),
        check_vma=False,
    )
```

```python
import functools
import math

import jax
import jax.numpy as jnp
from jax import lax
from jax.experimental import pallas as pl
from jax.experimental.pallas import tpu as pltpu
from jax.sharding import PartitionSpec as P


LOOKBACK = 6
NEG_FILL = -1e30
LOG2_E = math.log2(math.e)
SLACK_BYTES = 6 << 20


def stages(devices):
    seats = [0, 1, devices // 2, devices // 2 + 1]
    lanes = [2 * step for step in range(devices // 4)]
    return seats, lanes


def places_of(devices):
    seats, lanes = stages(devices)
    return [(i, j, lane + seat) for i, lane in enumerate(lanes) for j, seat in enumerate(seats)]


def run_all(copies):
    for copy in copies:
        copy.start()
    for copy in copies:
        copy.wait()


def piece(pieces, lanes_first, i, j, devices):
    seats, lanes = stages(devices)
    firsts = len(lanes) if lanes_first else len(seats)
    near, far = (i, j) if lanes_first else (j, i)
    return pieces[firsts + far - 1].at[near] if far else pieces[near].at[0]


def position(place, other, blocks):
    mask = place ^ other
    return lax.rem(mask, blocks) // 2, lax.rem(mask, 2) + 2 * (mask // blocks)


def pack_kernel(copies, lanes_first, place_ref, first_ref, second_ref, *refs):
    sems = refs[-1]
    width = refs[0].shape[-1]
    started = []
    for index, (i, j, mask) in enumerate(places_of(sems.shape[0])):
        head = (place_ref[0] ^ mask) // copies
        columns = pl.ds(pl.multiple_of(head * width, width), width)
        target = refs[i].at[j] if lanes_first else refs[j].at[i]
        for kind, source in enumerate((first_ref, second_ref)):
            started.append(pltpu.make_async_copy(source.at[:, columns], target.at[kind], sems.at[index, kind]))
    run_all(started)


def unpack_kernel(copies, counts, place_ref, *refs):
    sems, home_b, home_a, sums = refs[-1], refs[-2], refs[-3], refs[-4]
    outs = refs[-7:-4]
    devices = sems.shape[0]
    width = home_a.shape[2]
    half = outs[0].shape[0] // 2
    started = []
    for part, home in enumerate((home_a, home_b)):
        pieces = refs[: counts[0]] if part == 0 else refs[counts[0] : counts[0] + counts[1]]
        window = pl.ds(part * half, half)
        for index, (i, j, mask) in enumerate(places_of(devices)):
            source = piece(pieces, part == 0, i, j, devices)
            other = place_ref[0] ^ mask
            if copies > 1:
                started.append(pltpu.make_async_copy(source, home.at[other], sems.at[index, 3 * part]))
                continue
            columns = pl.ds(pl.multiple_of(other * width, width), width)
            for kind, out in enumerate(outs):
                rows = source.at[pl.ds(kind * half, half)]
                copy = pltpu.make_async_copy(rows, out.at[window, columns], sems.at[index, 3 * part + kind])
                started.append(copy)
    run_all(started)
    if copies > 1:
        for part, home in enumerate((home_a, home_b)):
            for head in range(devices // copies):
                columns = pl.ds(head * width, width)
                for kind in range(3):
                    rows = pl.ds(kind * half, half)
                    value = home[head * copies, rows].astype(jnp.float32)
                    for other in range(1, copies):
                        value = value + home[head * copies + other, rows].astype(jnp.float32)
                    sums[kind, part * half : (part + 1) * half, columns] = value.astype(sums.dtype)
        run_all([pltpu.make_async_copy(sums.at[kind], out, sems.at[0, kind]) for kind, out in enumerate(outs)])


def dot(left, right, contract):
    return lax.dot_general(left, right, (contract, ((), ())), preferred_element_type=jnp.float32)


def fold(tile, op):
    return op(tile.reshape(tile.shape[0] // 8, 8, tile.shape[1]), axis=0)


def pair(ref, place, block, kind, lanes_first):
    blocks = 2 * ref.shape[1 if not lanes_first else 0]
    parts = []
    for c in range(2):
        i, j = position(place, c * blocks + block, blocks)
        parts.append(ref[i, j, kind] if lanes_first else ref[j, i, kind])
    return jnp.concatenate(parts, axis=0)


def tile_count(blocks):
    return sum(min(block, LOOKBACK) + 1 for block in range(blocks))


def group_size(blocks):
    early = min(LOOKBACK, blocks)
    return 2 if early % 2 == 0 and (blocks - early) % 2 == 0 else 1


def for_groups(length, rows, blocks, on_group, off_group=None):
    early = min(LOOKBACK, blocks)
    group = group_size(blocks)
    visited = jnp.minimum(((length + group * rows - 1) // (group * rows)) * group, blocks)

    def either(members, higher):
        pl.when(members[0][0] < visited)(lambda: on_group(members, higher))
        if off_group is not None:
            pl.when(members[0][0] >= visited)(lambda: off_group(members, higher))

    def late(start, higher):
        members = [(start + k, tile_count(LOOKBACK) + (start + k - LOOKBACK) * (LOOKBACK + 1)) for k in range(group)]
        either([(block, base, LOOKBACK + 1) for block, base in members], higher)

    higher = None
    if blocks > early:
        late(blocks - group, None)

        def step(index, carried):
            start = blocks - (index + 1) * group
            late(start, [start + group + k for k in range(group)])
            return carried

        lax.fori_loop(1, (blocks - early) // group, step, 0)
        higher = [early + k for k in range(group)]
    for start in range(early - group, -1, -group):
        either([(block, tile_count(block), block + 1) for block in range(start, start + group)], higher)
        higher = [start + k for k in range(group)]


def stats_kernel(copies, length_ref, place_ref, bias_ref, qk_ref, kt_ref, power_ref, inverse_ref):
    rows, width = qk_ref.shape[3:]
    blocks = 2 * qk_ref.shape[1]
    both = 2 * rows
    log2_scale = LOG2_E / math.sqrt(width)
    place = place_ref[0]
    bias = bias_ref[place // copies] * LOG2_E
    part = place % copies
    length = length_ref[0]

    column = lax.broadcasted_iota(jnp.int32, (1, both), 1)
    own = [jnp.where((column // rows) == c, 0.0, bias) for c in range(2)]
    key_row = lax.broadcasted_iota(jnp.int32, (rows, both), 0)
    query_column = lax.broadcasted_iota(jnp.int32, (rows, both), 1) % rows
    for block in range(blocks):
        kt_ref[block] = pair(qk_ref, place, block, 1, False).T

    def on_group(members, higher):
        shifts = []
        for block, base, tiles in members:
            queries = pair(qk_ref, place, block, 0, False)
            first = block - (tiles - 1)
            peaks = [jnp.full((8, both), NEG_FILL, jnp.float32)] * 2
            for t in range(tiles):
                raw = dot(pair(qk_ref, place, first + t, 1, False), queries, ((1,), (1,)))
                for c in range(2):
                    tile = raw[c * rows : (c + 1) * rows]
                    if t == tiles - 1:
                        tile = jnp.where(key_row <= query_column, tile, NEG_FILL)
                    if tiles == LOOKBACK + 1 and t == 0:
                        tile = jnp.where(key_row > query_column, tile, NEG_FILL)
                    power_ref[base + t, c * rows : (c + 1) * rows] = tile
                    peaks[c] = jnp.maximum(peaks[c], fold(tile, jnp.max))
            peaks = [jnp.max(peaks[c], axis=0, keepdims=True) * log2_scale + own[c] for c in range(2)]
            peak = jnp.maximum(peaks[0], peaks[1])
            shifts.append([own[c] - peak for c in range(2)])
        for (block, base, tiles), shift in zip(members, shifts):
            total = jnp.zeros((8, both), jnp.float32)
            for t in range(tiles):
                for c in range(2):
                    window = slice(c * rows, (c + 1) * rows)
                    power = jnp.exp2(power_ref[base + t, window] * log2_scale + shift[c])
                    power_ref[base + t, window] = power
                    total = total + fold(power, jnp.sum)
            total = jnp.sum(total, axis=0, keepdims=True)
            live = block * rows + column % rows < length
            if copies > 1:
                live = live & ((column * copies) // both == part)
            inverse_ref[block] = jnp.broadcast_to(jnp.where(live, 1.0 / total, 0.0), (8, both))

    for_groups(length, rows, blocks, on_group)


def grads_kernel(
    copies, length_ref, place_ref, qk_ref, kt_ref, power_ref, inverse_ref, gv_ref, out_a, out_b, bias_ref, d_ref, dk_ref, dv_ref, bias_acc
):
    rows, width = gv_ref.shape[3:]
    blocks = 2 * gv_ref.shape[0]
    both = 2 * rows
    half = rows // 2
    root_scale = 1.0 / math.sqrt(width)
    place = place_ref[0]
    bias_acc[...] = jnp.zeros_like(bias_acc)

    def put(kind, block, tile):
        for c in range(2):
            i, j = position(place, c * blocks + block, blocks)
            out_a[i, j, kind * half : (kind + 1) * half] = tile[c * rows : c * rows + half]
            out_b[j, i, kind * half : (kind + 1) * half] = tile[c * rows + half : (c + 1) * rows]

    def key_blocks(members):
        for block in members or ():
            put(1, block, (dk_ref[block] * root_scale).astype(out_a.dtype))
            put(2, block, dv_ref[block].astype(out_a.dtype))

    def cleared(count):
        for block in range(count):
            dk_ref[block] = jnp.zeros(dk_ref.shape[1:], dk_ref.dtype)
            dv_ref[block] = jnp.zeros(dv_ref.shape[1:], dv_ref.dtype)

    def on_group(members, higher):
        if higher is None:
            cleared(members[0][0] - members[0][2] + 1)
        key_blocks(higher)
        deltas = []
        for k, (block, base, tiles) in enumerate(members):
            grads = pair(gv_ref, place, block, 0, True)
            first = block - (tiles - 1)
            moment = jnp.zeros((8, both), jnp.float32)
            for t in range(tiles):
                weight_grad = dot(pair(gv_ref, place, first + t, 1, True), grads, ((1,), (1,)))
                d_ref[k, t] = weight_grad
                moment = moment + fold(power_ref[base + t] * weight_grad, jnp.sum)
            deltas.append(jnp.sum(moment, axis=0, keepdims=True) * inverse_ref[block, :1])
        sums = []
        for k, (block, base, tiles) in enumerate(members):
            queries = pair(qk_ref, place, block, 0, False)
            grads = pair(gv_ref, place, block, 0, True)
            inverse = inverse_ref[block, :1]
            first = block - (tiles - 1)
            query_sum = jnp.zeros((width, both), jnp.float32)
            cross = jnp.zeros((8, rows), jnp.float32)
            for t in range(tiles):
                weights = power_ref[base + t] * inverse
                score_grad = weights * (d_ref[k, t] - deltas[k])
                cross = cross + fold(score_grad[:rows, rows:], jnp.sum) + fold(score_grad[rows:, :rows], jnp.sum)
                score_low = score_grad.astype(jnp.bfloat16)
                value_term = dot(weights.astype(jnp.bfloat16), grads, ((1,), (0,)))
                key_term = dot(score_low, queries, ((1,), (0,)))
                if higher is None and (k == 0 or t == tiles - 1):
                    dv_ref[first + t] = value_term
                    dk_ref[first + t] = key_term
                else:
                    dv_ref[first + t] += value_term
                    dk_ref[first + t] += key_term
                query_sum = query_sum + dot(kt_ref[first + t], score_low, ((1,), (0,)))
            bias_acc[...] += cross
            sums.append(query_sum)
        for (block, _, _), query_sum in zip(members, sums):
            put(0, block, (query_sum * root_scale).T.astype(out_a.dtype))

    def off_group(members, higher):
        if higher is None:
            cleared(blocks)
        key_blocks(higher)
        for block, _, _ in members:
            put(0, block, jnp.zeros((both, width), out_a.dtype))

    for_groups(length_ref[0], rows, blocks, on_group, off_group)
    key_blocks(range(group_size(blocks)))

    whole = jnp.sum(jnp.sum(bias_acc[...], axis=0, keepdims=True), axis=1, keepdims=True)
    lane = lax.broadcasted_iota(jnp.int32, bias_ref.shape, 1)
    bias_ref[...] = jnp.where(lane == place // copies, whole, 0.0)


def summed_over(value, axis):
    count = lax.axis_size(axis)
    if count & (count - 1):
        return lax.psum(value, axis)
    step = 1
    while step < count:
        pairs = [(source, source ^ step) for source in range(count)]
        value = value + lax.ppermute(value, axis, pairs)
        step *= 2
    return value


def in_hbm(value):
    return pltpu.with_memory_space_constraint(value, pltpu.HBM)


def moved(value, mask):
    devices = lax.axis_size("chan") * lax.axis_size("seq")
    return lax.ppermute(value, ("chan", "seq"), [(source, source ^ mask) for source in range(devices)])


def exchanged(by_lane, by_seat, devices):
    seats, lanes = stages(devices)
    first_a = [by_lane[0]] + [moved(by_lane[i], lanes[i]) for i in range(1, len(lanes))]
    first_b = [by_seat[0]] + [moved(by_seat[j], seats[j]) for j in range(1, len(seats))]
    last_b = []
    for i in range(1, len(lanes)):
        waiting, first_a[i] = lax.optimization_barrier((jnp.stack([value[i] for value in first_b]), first_a[i]))
        last_b.append(moved(waiting, lanes[i]))
    last_a = [moved(jnp.stack([value[j] for value in first_a]), seats[j]) for j in range(1, len(seats))]
    return first_a + last_a, first_b + last_b


def arranged(pieces, firsts):
    return jnp.stack([jnp.stack([value[0] for value in pieces[:firsts]])] + list(pieces[firsts:]))


def layer(queries, keys, values, out_grad, cross_bias, lengths):
    rows, features = queries.shape[2:]
    heads = cross_bias.shape[0]
    width = features // heads
    blocks = lax.axis_size("seq")
    devices = lax.axis_size("chan") * blocks
    copies = devices // heads
    seats, lanes = stages(devices)
    place = lax.axis_index("chan") * blocks + lax.axis_index("seq")
    places = place.astype(jnp.int32)[None]
    kind = queries.dtype
    both = 2 * rows
    tiles = min(LOOKBACK + 1, blocks)
    vmem = pl.BlockSpec(memory_space=pltpu.VMEM)
    smem = pl.BlockSpec(memory_space=pltpu.SMEM)
    anywhere = pl.BlockSpec(memory_space=pl.ANY)
    hbm = pl.BlockSpec(memory_space=pltpu.HBM)

    def by_lane(*block):
        return [jax.ShapeDtypeStruct((len(seats),) + block, kind)] * len(lanes)

    def by_seat(*block):
        return [jax.ShapeDtypeStruct((len(lanes),) + block, kind)] * len(seats)

    def size(*shapes):
        return sum(math.prod(shape.shape) * shape.dtype.itemsize for shape in shapes)

    def call(kernel, out_shape, in_specs, out_specs, scratch, grant, matmuls, args):
        flops = 2 * matmuls * tile_count(blocks) * both * both * width
        return pl.pallas_call(
            kernel,
            out_shape=out_shape,
            in_specs=in_specs,
            out_specs=out_specs,
            scratch_shapes=scratch,
            compiler_params=pltpu.CompilerParams(vmem_limit_bytes=grant + SLACK_BYTES),
            cost_estimate=pl.CostEstimate(flops=flops, bytes_accessed=2 << 20, transcendentals=0),
        )(*args)

    def pack(lanes_first, first, second):
        sends = by_lane(2, rows, width) if lanes_first else by_seat(2, rows, width)
        return call(
            functools.partial(pack_kernel, copies, lanes_first),
            sends,
            [smem, hbm, hbm],
            [vmem] * len(sends),
            [pltpu.SemaphoreType.DMA((devices, 2))],
            0,
            0,
            (places, in_hbm(first[0, 0]), in_hbm(second[0, 0])),
        )

    sent_a = pack(True, queries, keys)
    values, out_grad, sent_a = lax.optimization_barrier((values, out_grad, sent_a))
    sent_b = pack(False, out_grad, values)
    arrived_a, arrived_b = exchanged(sent_a, sent_b, devices)
    qk, gv = arranged(arrived_a, len(lanes)), arranged(arrived_b, len(seats))

    half = rows // 2
    group = group_size(blocks)
    turned_shape = jax.ShapeDtypeStruct((blocks, width, both), kind)
    power_shape = jax.ShapeDtypeStruct((tile_count(blocks), both, both), jnp.float32)
    inverse_shape = jax.ShapeDtypeStruct((blocks, 8, both), jnp.float32)
    sums_shape = jax.ShapeDtypeStruct((blocks, both, width), jnp.float32)
    d_shape = jax.ShapeDtypeStruct((group, tiles, both, both), jnp.float32)
    made = call(
        functools.partial(stats_kernel, copies),
        (turned_shape, power_shape, inverse_shape),
        [smem, smem, smem, vmem],
        [vmem] * 3,
        [],
        size(qk, turned_shape, power_shape, inverse_shape),
        1,
        (lengths, places, cross_bias, qk),
    )
    sends = (
        jax.ShapeDtypeStruct((len(lanes), len(seats), 3 * half, width), kind),
        jax.ShapeDtypeStruct((len(seats), len(lanes), 3 * half, width), kind),
        jax.ShapeDtypeStruct((1, heads), jnp.float32),
    )
    held = (d_shape, sums_shape, sums_shape)
    back_a, back_b, bias_sum = call(
        functools.partial(grads_kernel, copies),
        sends,
        [smem, smem] + [vmem] * 5,
        [vmem] * 3,
        [pltpu.VMEM(shape.shape, shape.dtype) for shape in held] + [pltpu.VMEM((8, rows), jnp.float32)],
        size(*held, *sends, qk, gv, turned_shape, power_shape, inverse_shape),
        4,
        (lengths, places, qk, *made, gv),
    )
    arrived_a, arrived_b = exchanged(list(back_a), list(back_b), devices)

    bias_out = summed_over(bias_sum[0], "dp")
    mask = 1
    while mask < devices:
        bias_out = bias_out + moved(bias_out, mask)
        mask *= 2

    flat = jax.ShapeDtypeStruct((rows, features), kind)
    alone = copies == 1
    arrived = arrived_a + arrived_b
    grads = pl.pallas_call(
        functools.partial(unpack_kernel, copies, (len(arrived_a), len(arrived_b))),
        out_shape=(flat, flat, flat),
        in_specs=[smem] + [anywhere] * len(arrived),
        out_specs=(hbm, hbm, hbm),
        scratch_shapes=[
            pltpu.VMEM((3, 16 if alone else rows, features), kind),
            pltpu.VMEM((1 if alone else devices,) + arrived_a[0].shape[1:], kind),
            pltpu.VMEM((1 if alone else devices,) + arrived_b[0].shape[1:], kind),
            pltpu.SemaphoreType.DMA((devices, 6)),
        ],
        compiler_params=pltpu.CompilerParams(vmem_limit_bytes=2 * SLACK_BYTES),
        name="unpack",
    )(places, *arrived)
    return tuple(grad[None, None] for grad in grads) + (bias_out,)


def solution(mesh):
    placed = P("dp", "chan", "seq", None)
    return jax.shard_map(
        layer,
        mesh=mesh,
        in_specs=(placed, placed, placed, placed, P(), P("dp")),
        out_specs=(placed, placed, placed, P()),
        check_vma=False,
    )
```
